32 devices in a mesh: section: 4 (over z), dp: 4 (over y, x), tensor: 2 (over core).
Axes of the slice: x: 2, y: 2, z: 4, core: 2. Of those that a mesh axis runs over, the one named last changes fastest.
Arguments:
- sent_out: bfloat16 [4, 2, 768, 4096], P('section', None, 'dp', 'tensor'), may hold values from -6 to 6
- sent_back: bfloat16 [4, 2, 768, 4096], P('section', None, 'dp', 'tensor'), may hold values from -6 to 6
- sent_grad: bfloat16 [4, 2, 768, 4096], P('section', None, 'dp', 'tensor'), may hold values from -6 to 6
- lengths: int32 [4, 4], P('section', 'dp'), may hold values from 48 to 192
- weight: bfloat16 [4, 4096, 4096], P('section', 'dp', 'tensor'), may hold values from -0.09375 to 0.09375
Outputs:
- emitted: bfloat16 [4, 2, 768, 4096], P('section', None, 'dp', 'tensor')
- rebuilt: bfloat16 [4, 2, 768, 4096], P('section', None, 'dp', 'tensor')
- input_grad: bfloat16 [4, 2, 768, 4096], P('section', None, 'dp', 'tensor')
- weight_grad: bfloat16 [4, 4096, 4096], P('section', 'dp', 'tensor')
The draws below stay inside these ranges and needn't reach their ends.
All inputs are finite; a program needn't handle non-finite values.
Results may differ from the reference program's by a relative error of at most 0.0075.
Values may be sent and summed in bfloat16 or wider, within the bound.
A program may use at most 128 MiB of HBM per device.

```python
import jax
import jax.numpy as jnp
from jax import lax

HALF = 4096
TOK = 192
SECTIONS = 4
REPLICAS = 4
ROWS = 768
N_TENSOR = 2


def set_ends(array, stream_key, low, top_value):
    dims = array.shape
    place = [jax.random.randint(jax.random.fold_in(stream_key, axis), (), 0, dims[axis]) for axis in range(len(dims))]
    array = array.at[tuple(place)].set(low)
    longest = dims.index(max(dims))
    place[longest] = (place[longest] + 1) % dims[longest]
    return array.at[tuple(place)].set(top_value)


def block_levels(key, shape, cuts, least, high):
    gain, own = 1.0, jax.random.fold_in(key, 6)
    for dim, shards_of in cuts:
        steps = jnp.exp(jax.random.uniform(jax.random.fold_in(own, dim), (shards_of,), jnp.float32, least / len(cuts), high / len(cuts)))
        gain = gain * jnp.repeat(steps, shape[dim] // shards_of).reshape([-1 if axis == dim else 1 for axis in range(len(shape))])
    return gain


def centred(rng, dims, deviation, most, pieces=(), kind=jnp.bfloat16):
    result = deviation * jax.random.normal(rng, dims, jnp.float32)
    if pieces:
        result = result * block_levels(rng, dims, pieces, -0.22, 0.18)
    return jnp.clip(result, -most, most).astype(kind)


def setup_inputs(seed: int = 0) -> dict:
    arg_keys = jax.random.split(jax.random.key(seed), 6)
    return {
        "sent_out": centred(arg_keys[0], (SECTIONS, 2, ROWS, HALF), 1.0, 6.0, ((0, 4), (2, 4), (3, 2))),
        "sent_back": centred(arg_keys[1], (SECTIONS, 2, ROWS, HALF), 1.0, 6.0, ((0, 4), (2, 4), (3, 2))),
        "sent_grad": centred(arg_keys[2], (SECTIONS, 2, ROWS, HALF), 1.0, 6.0, ((0, 4), (2, 4), (3, 2))),
        "lengths": set_ends(jax.random.randint(arg_keys[3], (SECTIONS, REPLICAS), TOK // 4, TOK + 1), jax.random.fold_in(arg_keys[3], 1), TOK // 4, TOK).astype(jnp.int32),
        "weight": centred(arg_keys[4], (SECTIONS, HALF, HALF), HALF ** -0.5, 0.09375, ((0, 4), (1, 4), (2, 2))),
    }


def across_rows(left, right):
    return lax.dot_general(left, right, (((0,), (0,)), ((), ())), preferred_element_type=jnp.float32)


def slope(hidden):
    sigma = jax.nn.sigmoid(hidden)
    return sigma * (1.0 + hidden * (1.0 - sigma))


def grouped_back(hidden, weights):
    count = hidden.shape[0]
    blocks = hidden.astype(jnp.float32).reshape(count, N_TENSOR, -1)
    tables = weights.astype(jnp.float32).reshape(weights.shape[0], N_TENSOR, -1)
    parts = jnp.einsum("rkc,jkc->krj", blocks, tables)
    return jnp.sum(parts.astype(jnp.bfloat16).astype(jnp.float32), axis=0)


def reference(sent_out, sent_back, sent_grad, lengths, weight):
    inbound = jnp.roll(sent_out, 1, axis=0)
    back = jnp.roll(sent_back, -1, axis=0)
    incoming = jnp.roll(sent_grad, -1, axis=0)
    total_rows = sent_out.shape[2]
    position = jnp.arange(total_rows, dtype=jnp.int32) % TOK
    replica = jnp.arange(total_rows, dtype=jnp.int32) // TOK
    zero = jnp.zeros((), jnp.bfloat16)
    emitted, rebuilt, input_grad, weight_grad = [], [], [], []
    for section_index in range(SECTIONS):
        matrix = weight[section_index]
        upper_in, lower_in = inbound[section_index, 0], inbound[section_index, 1]
        pre = jnp.dot(upper_in, matrix, preferred_element_type=jnp.float32)
        upper_out = (lower_in.astype(jnp.float32) + jax.nn.silu(pre)).astype(jnp.bfloat16)
        emitted.append(jnp.stack([upper_out, upper_in]))
        back_upper, back_lower = back[section_index, 0], back[section_index, 1]
        pre_held = jnp.dot(back_lower, matrix, preferred_element_type=jnp.float32)
        rebuilt_lower = (back_upper.astype(jnp.float32) - jax.nn.silu(pre_held)).astype(jnp.bfloat16)
        rebuilt.append(jnp.stack([back_lower, rebuilt_lower]))
        limit = lengths[section_index][replica]
        keep = (position < limit)[:, None]
        dupper = jnp.where(keep, incoming[section_index, 0], zero)
        dlower = jnp.where(keep, incoming[section_index, 1], zero)
        hidden = (dupper.astype(jnp.float32) * slope(pre_held)).astype(jnp.bfloat16)
        dupper_in = (dlower.astype(jnp.float32) + grouped_back(hidden, matrix)).astype(jnp.bfloat16)
        input_grad.append(jnp.stack([dupper_in, dupper]))
        weight_grad.append(across_rows(back_lower, hidden).astype(jnp.bfloat16))
    return (jnp.stack(emitted), jnp.stack(rebuilt), jnp.stack(input_grad), jnp.stack(weight_grad))
```

```python
import jax
import jax.numpy as jnp
from jax import lax
from jax.sharding import PartitionSpec as P


def shifted(block, axis, distance):
    devices = range(lax.axis_size(axis))
    route = [((i - distance) % len(devices), i) for i in devices]
    return lax.ppermute(block, axis, route)


def across_rows(left, right):
    return lax.dot_general(
        left, right, (((0,), (0,)), ((), ())), preferred_element_type=jnp.float32
    )


def slope(hidden):
    sigma = jax.nn.sigmoid(hidden)
    return sigma * (1.0 + hidden * (1.0 - sigma))


def local(sent_out, sent_back, sent_grad, lengths, weight):
    token_rows = sent_out.shape[2]
    own_weight = weight[0]

    def shares(block):
        full = lax.all_gather(block, "tensor", axis=1, tiled=True)
        return lax.all_to_all(full, "dp", split_axis=1, concat_axis=0, tiled=True)

    def project(share):
        partial = jnp.dot(share, own_weight, preferred_element_type=jnp.float32)
        return lax.psum_scatter(
            partial.astype(jnp.bfloat16), "dp", scatter_dimension=0, tiled=True
        ).astype(jnp.float32)

    back_lower = shifted(sent_back[0, 1], "section", -1)
    upper_in = shifted(sent_out[0, 0], "section", 1)
    incoming_upper = shifted(sent_grad[0, 0], "section", -1)
    lower_in = shifted(sent_out[0, 1], "section", 1)
    back_upper = shifted(sent_back[0, 0], "section", -1)
    incoming_lower = shifted(sent_grad[0, 1], "section", -1)

    held_share = shares(back_lower)
    pre_held = project(held_share)
    keep = (jnp.arange(token_rows, dtype=jnp.int32) < lengths[0, 0])[:, None]
    zero = jnp.zeros((), jnp.bfloat16)
    dupper = jnp.where(keep, incoming_upper, zero)
    dlower = jnp.where(keep, incoming_lower, zero)
    hidden = (dupper.astype(jnp.float32) * slope(pre_held)).astype(jnp.bfloat16)
    hidden_all = lax.all_gather(hidden, "dp", axis=0, tiled=True)
    rebuilt_lower = (back_upper.astype(jnp.float32) - jax.nn.silu(pre_held)).astype(jnp.bfloat16)
    rebuilt = jnp.stack([back_lower, rebuilt_lower])[None]

    pre = project(shares(upper_in))
    upper_out = (lower_in.astype(jnp.float32) + jax.nn.silu(pre)).astype(jnp.bfloat16)
    emitted = jnp.stack([upper_out, upper_in])[None]

    terms = lax.dot_general(
        hidden_all, own_weight, (((1,), (1,)), ((), ())), preferred_element_type=jnp.float32
    ).astype(jnp.bfloat16)
    terms = lax.all_to_all(terms, "dp", split_axis=0, concat_axis=1, tiled=True)
    through = lax.psum_scatter(terms, "tensor", scatter_dimension=1, tiled=True).astype(jnp.float32)
    dupper_in = (dlower.astype(jnp.float32) + through).astype(jnp.bfloat16)
    grads_out = jnp.stack([dupper_in, dupper])[None]
    weight_grad = across_rows(held_share, hidden_all).astype(jnp.bfloat16)[None]
    return (emitted, rebuilt, grads_out, weight_grad)


def solution(mesh):
    return jax.shard_map(
        local,
        mesh=mesh,
        in_specs=(
            P("section", None, "dp", "tensor"),
            P("section", None, "dp", "tensor"),
            P("section", None, "dp", "tensor"),
            P("section", "dp"),
            P("section", "dp", "tensor"),
        ),
        out_specs=(
            P("section", None, "dp", "tensor"),
            P("section", None, "dp", "tensor"),
            P("section", None, "dp", "tensor"),
            P("section", "dp", "tensor"),
        ),
        check_vma=False,
    )
```

```python
import functools

import jax
import jax.numpy as jnp
from jax import lax
from jax.experimental import pallas as pl
from jax.experimental.pallas import tpu as pltpu
from jax.sharding import PartitionSpec as P


def shifted(block, axis, distance):
    devices = range(lax.axis_size(axis))
    route = [((i - distance) % len(devices), i) for i in devices]
    return lax.ppermute(block, axis, route)


def across_rows(left, right):
    return lax.dot_general(
        left, right, (((0,), (0,)), ((), ())), preferred_element_type=jnp.float32
    )


def slope(hidden):
    sigma = jax.nn.sigmoid(hidden)
    return sigma * (1.0 + hidden * (1.0 - sigma))


def spread(sent_out, sent_back, sent_grad, lengths, weight):
    token_rows = sent_out.shape[2]
    own_weight = weight[0]

    def shares(block):
        full = lax.all_gather(block, "tensor", axis=1, tiled=True)
        return lax.all_to_all(full, "dp", split_axis=1, concat_axis=0, tiled=True)

    def project(share):
        partial = jnp.dot(share, own_weight, preferred_element_type=jnp.float32)
        return lax.psum_scatter(
            partial.astype(jnp.bfloat16), "dp", scatter_dimension=0, tiled=True
        ).astype(jnp.float32)

    back_lower = shifted(sent_back[0, 1], "section", -1)
    upper_in = shifted(sent_out[0, 0], "section", 1)
    incoming_upper = shifted(sent_grad[0, 0], "section", -1)
    lower_in = shifted(sent_out[0, 1], "section", 1)
    back_upper = shifted(sent_back[0, 0], "section", -1)
    incoming_lower = shifted(sent_grad[0, 1], "section", -1)

    held_share = shares(back_lower)
    pre_held = project(held_share)
    keep = (jnp.arange(token_rows, dtype=jnp.int32) < lengths[0, 0])[:, None]
    zero = jnp.zeros((), jnp.bfloat16)
    dupper = jnp.where(keep, incoming_upper, zero)
    dlower = jnp.where(keep, incoming_lower, zero)
    hidden = (dupper.astype(jnp.float32) * slope(pre_held)).astype(jnp.bfloat16)
    hidden_all = lax.all_gather(hidden, "dp", axis=0, tiled=True)
    rebuilt_lower = (back_upper.astype(jnp.float32) - jax.nn.silu(pre_held)).astype(jnp.bfloat16)
    rebuilt = jnp.stack([back_lower, rebuilt_lower])[None]

    pre = project(shares(upper_in))
    upper_out = (lower_in.astype(jnp.float32) + jax.nn.silu(pre)).astype(jnp.bfloat16)
    emitted = jnp.stack([upper_out, upper_in])[None]

    terms = lax.dot_general(
        hidden_all, own_weight, (((1,), (1,)), ((), ())), preferred_element_type=jnp.float32
    ).astype(jnp.bfloat16)
    terms = lax.all_to_all(terms, "dp", split_axis=0, concat_axis=1, tiled=True)
    through = lax.psum_scatter(terms, "tensor", scatter_dimension=1, tiled=True).astype(jnp.float32)
    dupper_in = (dlower.astype(jnp.float32) + through).astype(jnp.bfloat16)
    grads_out = jnp.stack([dupper_in, dupper])[None]
    weight_grad = across_rows(held_share, hidden_all).astype(jnp.bfloat16)[None]
    return (emitted, rebuilt, grads_out, weight_grad)


MESH = pl.DeviceIdType.MESH
BACK_LOWER, GRAD_UPPER, BACK_UPPER, GRAD_LOWER, OUT_UPPER, OUT_LOWER = range(6)


def step_kernel(
    lengths, sent_out, sent_back, sent_grad, weight,
    emitted, rebuilt, grads_out, weight_grad,
    w, got, share, part, summed, hidden, terms, tx, trx, ts, tr, stage, wg,
    z_send, z_recv, d_send, d_recv, r_send, r_recv, p_send, p_recv,
    h_send, h_recv, t_send, t_recv, f_send, f_recv, w_sem, o_sem,
):
    f32, bf16 = jnp.float32, jnp.bfloat16
    n_s, n_d, n_t = (lax.axis_size(a) for a in ("section", "dp", "tensor"))
    me_s, me_d, me_t = (lax.axis_index(a) for a in ("section", "dp", "tensor"))
    rows, local_features = got.shape[1], got.shape[2]
    half, depth = share.shape[3], share.shape[4]
    per = local_features // depth
    other = 1 - me_t
    nxt, prv = lax.rem(me_s + 1, n_s), lax.rem(me_s + n_s - 1, n_s)

    def replica(k):
        return lax.rem(me_d + k + n_d, n_d)

    barrier = pltpu.get_barrier_semaphore()
    for k in range(n_d):
        for c in range(n_t):
            if k or c:
                pl.semaphore_signal(
                    barrier, inc=1, device_id=(me_s, replica(k), lax.rem(me_t + c, n_t)), device_id_type=MESH
                )
    for z in (nxt, prv):
        pl.semaphore_signal(barrier, inc=1, device_id=(z, me_d, me_t), device_id_type=MESH)
    pl.semaphore_wait(barrier, n_d * n_t - 1 + 2)

    def remote(src, dst, send, recv, where):
        return pltpu.make_async_remote_copy(
            src_ref=src, dst_ref=dst, send_sem=send, recv_sem=recv, device_id=where, device_id_type=MESH
        )

    def landed(dst, sem):
        pltpu.make_async_copy(dst, dst, sem).wait()

    def along_z(i):
        src, piece, z = {
            BACK_LOWER: (sent_back, 1, prv), BACK_UPPER: (sent_back, 0, prv),
            GRAD_UPPER: (sent_grad, 0, prv), GRAD_LOWER: (sent_grad, 1, prv),
            OUT_UPPER: (sent_out, 0, nxt), OUT_LOWER: (sent_out, 1, nxt),
        }[i]
        return remote(src.at[0, piece], got.at[i], z_send.at[i], z_recv.at[i], (z, me_d, me_t))

    along_z(BACK_LOWER).start()
    w_copy = pltpu.make_async_copy(weight.at[0], w, w_sem)
    w_copy.start()
    along_z(GRAD_UPPER).start()
    along_z(BACK_UPPER).start()
    along_z(GRAD_LOWER).start()

    def deal(i, x, finish):
        for h in range(n_t):
            for j in range(per):
                n = h * per + j
                target = me_t * per + j
                src = got.at[i, pl.ds(h * half, half), pl.ds(j * depth, depth)]
                dst = share.at[x, me_d, h]
                own = jnp.logical_and(target == me_d, me_t == h)

                @pl.when(own)
                def _():
                    if not finish:
                        pltpu.make_async_copy(src, dst, d_recv.at[x, me_d]).start()

                @pl.when(jnp.logical_not(own))
                def _():
                    copy = remote(src, dst, d_send.at[x, n], d_recv.at[x, me_d], (me_s, target, h))
                    if finish:
                        copy.wait_send()
                    else:
                        copy.start()

    def relay(x, k):
        r = replica(k)
        return remote(
            share.at[x, r, me_t], share.at[x, r, me_t], r_send.at[x, r], r_recv.at[x, r], (me_s, me_d, other)
        )

    def partial(x, k):
        r = replica(k)
        return remote(
            part.at[x, r], summed.at[x, k - 1], p_send.at[x, k - 1], p_recv.at[x, k - 1], (me_s, r, me_t)
        )

    def gather(x):
        for k in range(n_d):
            landed(share.at[x, replica(k), me_t], d_recv.at[x, replica(k)])
            relay(x, k).start()
        for k in range(n_d):
            landed(share.at[x, replica(k), other], r_recv.at[x, replica(k)])

    def multiply(x, send):
        for k in list(range(1, n_d)) + [0]:
            r = replica(k)

            @pl.loop(0, local_features // 512)
            def _(c):
                cols = pl.ds(pl.multiple_of(c * 512, 512), 512)
                left = share[x, r].reshape(rows, depth)
                part[x, r, :, cols] = jnp.dot(left, w[:, cols], preferred_element_type=f32).astype(bf16)

            if send and k:
                partial(x, k).start()

    def total(x, cols):
        pre = part[x, me_d, :, cols].astype(f32)
        for k in range(n_d - 1):
            pre = pre + summed[x, k, :, cols].astype(f32)
        return pre

    def tiles(body):
        @pl.loop(0, local_features // 256)
        def _(c):
            body(pl.ds(pl.multiple_of(c * 256, 256), 256))

    def out(i, src, dst):
        return pltpu.make_async_copy(src, dst, o_sem.at[i])

    outs = [
        out(0, got.at[BACK_LOWER], rebuilt.at[0, 0]),
        out(1, got.at[OUT_UPPER], emitted.at[0, 1]),
        out(2, stage.at[0], grads_out.at[0, 1]),
        out(3, stage.at[1], rebuilt.at[0, 1]),
        out(4, stage.at[2], emitted.at[0, 0]),
        out(5, stage.at[3], grads_out.at[0, 0]),
        out(6, wg, weight_grad.at[0]),
    ]

    along_z(BACK_LOWER).wait_recv()
    along_z(OUT_UPPER).start()
    deal(BACK_LOWER, 0, False)
    outs[0].start()
    gather(0)
    w_copy.wait()
    multiply(0, True)

    along_z(OUT_UPPER).wait_recv()
    along_z(OUT_LOWER).start()
    deal(OUT_UPPER, 1, False)
    outs[1].start()
    gather(1)
    multiply(1, False)

    along_z(GRAD_UPPER).wait_recv()
    for k in range(1, n_d):
        partial(0, k).wait_recv()
    live = lengths[0, 0]

    def keep(block):
        place = lax.broadcasted_iota(jnp.int32, block.shape, 0)
        return jnp.where(place < live, block.astype(f32), 0.0)

    def hide(cols):
        pre = total(0, cols)
        dupper = keep(got[GRAD_UPPER, :, cols])
        stage[0, :, cols] = dupper.astype(bf16)
        sigma = jax.nn.sigmoid(pre)
        gated = (dupper * (sigma * (1.0 + pre * (1.0 - sigma)))).astype(bf16)
        hidden[me_d, :, :, cols] = gated.reshape(n_t, half, 256)

    tiles(hide)

    def show(k):
        return remote(
            hidden.at[me_d], hidden.at[me_d], h_send.at[k - 1], h_recv.at[k - 1], (me_s, replica(k), me_t)
        )

    for k in range(1, n_d):
        show(k).start()
    for k in range(1, n_d):
        partial(1, k).start()
    outs[2].start()

    along_z(BACK_UPPER).wait_recv()

    def rebuild(cols):
        pre = total(0, cols)
        upper = got[BACK_UPPER, :, cols].astype(f32)
        stage[1, :, cols] = (upper - pre * jax.nn.sigmoid(pre)).astype(bf16)

    tiles(rebuild)
    outs[3].start()

    for k in range(1, n_d):
        landed(hidden.at[replica(-k)], h_recv.at[k - 1])

    @pl.loop(0, depth // 256)
    def _(c):
        cols = pl.ds(pl.multiple_of(c * 256, 256), 256)
        left = hidden[...].reshape(n_d * rows, local_features)
        product = lax.dot_general(left, w[cols, :], (((1,), (1,)), ((), ())), preferred_element_type=f32)
        terms[:, :, :, cols] = product.reshape(n_d, n_t, half, 256)

    for r in range(n_d):
        tx[r] = terms[r, other].astype(bf16)
    swap = remote(tx, trx, t_send, t_recv, (me_s, me_d, other))
    swap.start()

    def weigh(lo, hi):
        @pl.loop(lo, hi)
        def _(c):
            cols = pl.ds(pl.multiple_of(c * 256, 256), 256)
            left = share[0, :, :, :, cols].reshape(n_d * rows, 256)
            right = hidden[...].reshape(n_d * rows, local_features)
            product = lax.dot_general(left, right, (((0,), (0,)), ((), ())), preferred_element_type=f32)
            wg[cols, :] = product.astype(bf16)

    swap.wait_recv()
    owner, place = lax.div(me_d, per), lax.rem(me_d, per)

    def back_to(k, finish):
        r = replica(k)
        src, dst = ts.at[r], tr.at[place, me_t]
        own = jnp.logical_and(k == 0, me_t == owner)

        @pl.when(own)
        def _():
            if not finish:
                pltpu.make_async_copy(src, dst, f_recv.at[place, me_t]).start()

        @pl.when(jnp.logical_not(own))
        def _():
            copy = remote(src, dst, f_send.at[k], f_recv.at[place, me_t], (me_s, r, owner))
            if finish:
                copy.wait_send()
            else:
                copy.start()

    for k in range(1, n_d + 1):
        r = replica(k)
        ts[r] = (terms[r, me_t] + trx[r].astype(f32)).astype(bf16)
        back_to(k % n_d, False)

    weigh(0, depth // 256)
    outs[6].start()

    along_z(OUT_LOWER).wait_recv()
    for k in range(1, n_d):
        partial(1, k).wait_recv()

    def emit(cols):
        pre = total(1, cols)
        lower = got[OUT_LOWER, :, cols].astype(f32)
        stage[2, :, cols] = (lower + pre * jax.nn.sigmoid(pre)).astype(bf16)

    tiles(emit)
    outs[4].start()

    along_z(GRAD_LOWER).wait_recv()
    for j in range(per):
        for h in range(n_t):
            landed(tr.at[j, h], f_recv.at[j, h])

    for j in range(per):
        span = pl.ds(j * depth, depth)
        through = tr[j].reshape(rows, depth).astype(f32)
        stage[3, :, span] = (keep(got[GRAD_LOWER, :, span]) + through).astype(bf16)
    outs[5].start()

    for i in range(6):
        along_z(i).wait_send()
    for x, i in ((0, BACK_LOWER), (1, OUT_UPPER)):
        deal(i, x, True)
        for k in range(n_d):
            relay(x, k).wait_send()
        for k in range(1, n_d):
            partial(x, k).wait_send()
    for k in range(1, n_d):
        show(k).wait_send()
    swap.wait_send()
    for k in range(n_d):
        back_to(k, True)
    for copy in outs:
        copy.wait()


def together(sizes, sent_out, sent_back, sent_grad, lengths, weight):
    n_d, n_t = sizes
    rows, features = sent_out.shape[2:]
    depth = weight.shape[1]
    half, per = rows // n_t, features // depth
    bf16 = jnp.bfloat16
    dma, vmem = pltpu.SemaphoreType.DMA, pltpu.VMEM
    anywhere = pl.BlockSpec(memory_space=pl.ANY)
    return pl.pallas_call(
        step_kernel,
        out_shape=[jax.ShapeDtypeStruct(a.shape, bf16) for a in (sent_out, sent_back, sent_grad, weight)],
        in_specs=[pl.BlockSpec(memory_space=pltpu.SMEM)] + [anywhere] * 4,
        out_specs=[anywhere] * 4,
        scratch_shapes=[
            vmem((depth, features), bf16),
            vmem((6, rows, features), bf16),
            vmem((2, n_d, n_t, half, depth), bf16),
            vmem((2, n_d, rows, features), bf16),
            vmem((2, n_d - 1, rows, features), bf16),
            vmem((n_d, n_t, half, features), bf16),
            vmem((n_d, n_t, half, depth), jnp.float32),
            vmem((n_d, half, depth), bf16),
            vmem((n_d, half, depth), bf16),
            vmem((n_d, half, depth), bf16),
            vmem((per, n_t, half, depth), bf16),
            vmem((4, rows, features), bf16),
            vmem((depth, features), bf16),
            dma((6,)), dma((6,)),
            dma((2, n_t * per)), dma((2, n_d)),
            dma((2, n_d)), dma((2, n_d)),
            dma((2, n_d - 1)), dma((2, n_d - 1)),
            dma((n_d - 1,)), dma((n_d - 1,)),
            dma(()), dma(()),
            dma((n_d,)), dma((per, n_t)),
            dma(()), dma((7,)),
        ],
        compiler_params=pltpu.CompilerParams(
            collective_id=0, has_side_effects=True, vmem_limit_bytes=62 * 2**20
        ),
    )(lengths, sent_out, sent_back, sent_grad, weight)


def local(sizes, sent_out, sent_back, sent_grad, lengths, weight):
    n_s, n_d, n_t = sizes
    rows, features = sent_out.shape[2:]
    depth = weight.shape[1]
    fits = n_s > 2 and n_t == 2 and rows % 32 == 0 and features % depth == 0 and depth % 256 == 0
    if fits and features % 512 == 0:
        return tuple(together((n_d, n_t), sent_out, sent_back, sent_grad, lengths, weight))
    return spread(sent_out, sent_back, sent_grad, lengths, weight)


def solution(mesh):
    return jax.shard_map(
        functools.partial(local, tuple(mesh.shape[a] for a in ("section", "dp", "tensor"))),
        mesh=mesh,
        in_specs=(
            P("section", None, "dp", "tensor"),
            P("section", None, "dp", "tensor"),
            P("section", None, "dp", "tensor"),
            P("section", "dp"),
            P("section", "dp", "tensor"),
        ),
        out_specs=(
            P("section", None, "dp", "tensor"),
            P("section", None, "dp", "tensor"),
            P("section", None, "dp", "tensor"),
            P("section", "dp", "tensor"),
        ),
        check_vma=False,
    )
```

```python
import functools

import jax
import jax.numpy as jnp
from jax import lax
from jax.experimental import pallas as pl
from jax.experimental.pallas import tpu as pltpu
from jax.sharding import PartitionSpec as P


def shifted(block, axis, distance):
    devices = range(lax.axis_size(axis))
    route = [((i - distance) % len(devices), i) for i in devices]
    return lax.ppermute(block, axis, route)


def across_rows(left, right):
    return lax.dot_general(
        left, right, (((0,), (0,)), ((), ())), preferred_element_type=jnp.float32
    )


def slope(hidden):
    sigma = jax.nn.sigmoid(hidden)
    return sigma * (1.0 + hidden * (1.0 - sigma))


def spread(sent_out, sent_back, sent_grad, lengths, weight):
    token_rows = sent_out.shape[2]
    own_weight = weight[0]

    def shares(block):
        full = lax.all_gather(block, "tensor", axis=1, tiled=True)
        return lax.all_to_all(full, "dp", split_axis=1, concat_axis=0, tiled=True)

    def project(share):
        partial = jnp.dot(share, own_weight, preferred_element_type=jnp.float32)
        return lax.psum_scatter(
            partial.astype(jnp.bfloat16), "dp", scatter_dimension=0, tiled=True
        ).astype(jnp.float32)

    back_lower = shifted(sent_back[0, 1], "section", -1)
    upper_in = shifted(sent_out[0, 0], "section", 1)
    incoming_upper = shifted(sent_grad[0, 0], "section", -1)
    lower_in = shifted(sent_out[0, 1], "section", 1)
    back_upper = shifted(sent_back[0, 0], "section", -1)
    incoming_lower = shifted(sent_grad[0, 1], "section", -1)

    held_share = shares(back_lower)
    pre_held = project(held_share)
    keep = (jnp.arange(token_rows, dtype=jnp.int32) < lengths[0, 0])[:, None]
    zero = jnp.zeros((), jnp.bfloat16)
    dupper = jnp.where(keep, incoming_upper, zero)
    dlower = jnp.where(keep, incoming_lower, zero)
    hidden = (dupper.astype(jnp.float32) * slope(pre_held)).astype(jnp.bfloat16)
    hidden_all = lax.all_gather(hidden, "dp", axis=0, tiled=True)
    rebuilt_lower = (back_upper.astype(jnp.float32) - jax.nn.silu(pre_held)).astype(jnp.bfloat16)
    rebuilt = jnp.stack([back_lower, rebuilt_lower])[None]

    pre = project(shares(upper_in))
    upper_out = (lower_in.astype(jnp.float32) + jax.nn.silu(pre)).astype(jnp.bfloat16)
    emitted = jnp.stack([upper_out, upper_in])[None]

    terms = lax.dot_general(
        hidden_all, own_weight, (((1,), (1,)), ((), ())), preferred_element_type=jnp.float32
    ).astype(jnp.bfloat16)
    terms = lax.all_to_all(terms, "dp", split_axis=0, concat_axis=1, tiled=True)
    through = lax.psum_scatter(terms, "tensor", scatter_dimension=1, tiled=True).astype(jnp.float32)
    dupper_in = (dlower.astype(jnp.float32) + through).astype(jnp.bfloat16)
    grads_out = jnp.stack([dupper_in, dupper])[None]
    weight_grad = across_rows(held_share, hidden_all).astype(jnp.bfloat16)[None]
    return (emitted, rebuilt, grads_out, weight_grad)


MESH = pl.DeviceIdType.MESH
BACK_LOWER, GRAD_UPPER, BACK_UPPER, GRAD_LOWER, OUT_UPPER, OUT_LOWER = range(6)


def step_kernel(
    lengths, sent_out, sent_back, sent_grad, weight,
    emitted, rebuilt, grads_out, weight_grad,
    w, got, share, part, summed, hidden, terms, tx, trx, ts, tr, stage, wg,
    z_send, z_recv, d_send, d_recv, r_send, r_recv, p_send, p_recv,
    h_send, h_recv, t_send, t_recv, f_send, f_recv, w_sem, o_sem,
):
    f32, bf16 = jnp.float32, jnp.bfloat16
    n_s, n_d, n_t = (lax.axis_size(a) for a in ("section", "dp", "tensor"))
    me_s, me_d, me_t = (lax.axis_index(a) for a in ("section", "dp", "tensor"))
    rows, local_features = got.shape[1], got.shape[2]
    half, depth = share.shape[3], share.shape[4]
    per = local_features // depth
    other = 1 - me_t
    nxt, prv = lax.rem(me_s + 1, n_s), lax.rem(me_s + n_s - 1, n_s)

    def replica(k):
        return lax.rem(me_d + k + n_d, n_d)

    barrier = pltpu.get_barrier_semaphore()
    for k in range(n_d):
        for c in range(n_t):
            if k or c:
                pl.semaphore_signal(
                    barrier, inc=1, device_id=(me_s, replica(k), lax.rem(me_t + c, n_t)), device_id_type=MESH
                )
    for z in (nxt, prv):
        pl.semaphore_signal(barrier, inc=1, device_id=(z, me_d, me_t), device_id_type=MESH)
    pl.semaphore_wait(barrier, n_d * n_t - 1 + 2)

    def remote(src, dst, send, recv, where):
        return pltpu.make_async_remote_copy(
            src_ref=src, dst_ref=dst, send_sem=send, recv_sem=recv, device_id=where, device_id_type=MESH
        )

    def landed(dst, sem):
        pltpu.make_async_copy(dst, dst, sem).wait()

    def along_z(i):
        src, piece, z = {
            BACK_LOWER: (sent_back, 1, prv), BACK_UPPER: (sent_back, 0, prv),
            GRAD_UPPER: (sent_grad, 0, prv), GRAD_LOWER: (sent_grad, 1, prv),
            OUT_UPPER: (sent_out, 0, nxt), OUT_LOWER: (sent_out, 1, nxt),
        }[i]
        return remote(src.at[0, piece], got.at[i], z_send.at[i], z_recv.at[i], (z, me_d, me_t))

    along_z(BACK_LOWER).start()
    w_copy = pltpu.make_async_copy(weight.at[0], w, w_sem)
    w_copy.start()

    def deal(i, x, finish):
        for h in range(n_t):
            for j in range(per):
                n = h * per + j
                target = me_t * per + j
                src = got.at[i, pl.ds(h * half, half), pl.ds(j * depth, depth)]
                dst = share.at[x, me_d, h]
                own = jnp.logical_and(target == me_d, me_t == h)

                @pl.when(own)
                def _():
                    if not finish:
                        pltpu.make_async_copy(src, dst, d_recv.at[x, me_d]).start()

                @pl.when(jnp.logical_not(own))
                def _():
                    copy = remote(src, dst, d_send.at[x, n], d_recv.at[x, me_d], (me_s, target, h))
                    if finish:
                        copy.wait_send()
                    else:
                        copy.start()

    def relay(x, k):
        r = replica(k)
        return remote(
            share.at[x, r, me_t], share.at[x, r, me_t], r_send.at[x, r], r_recv.at[x, r], (me_s, me_d, other)
        )

    def partial(x, k):
        r = replica(k)
        return remote(
            part.at[x, r], summed.at[x, k - 1], p_send.at[x, k - 1], p_recv.at[x, k - 1], (me_s, r, me_t)
        )

    def gather(x):
        for k in range(n_d):
            landed(share.at[x, replica(k), me_t], d_recv.at[x, replica(k)])
            relay(x, k).start()
        for k in range(n_d):
            landed(share.at[x, replica(k), other], r_recv.at[x, replica(k)])

    def multiply(x, send):
        for k in list(range(1, n_d)) + [0]:
            r = replica(k)

            @pl.loop(0, local_features // 512)
            def _(c):
                cols = pl.ds(pl.multiple_of(c * 512, 512), 512)
                left = share[x, r].reshape(rows, depth)
                part[x, r, :, cols] = jnp.dot(left, w[:, cols], preferred_element_type=f32).astype(bf16)

            if send and k:
                partial(x, k).start()

    def total(x, cols):
        pre = part[x, me_d, :, cols].astype(f32)
        for k in range(n_d - 1):
            pre = pre + summed[x, k, :, cols].astype(f32)
        return pre

    def tiles(body):
        @pl.loop(0, local_features // 256)
        def _(c):
            body(pl.ds(pl.multiple_of(c * 256, 256), 256))

    def out(i, src, dst):
        return pltpu.make_async_copy(src, dst, o_sem.at[i])

    outs = [
        out(0, got.at[BACK_LOWER], rebuilt.at[0, 0]),
        out(1, got.at[OUT_UPPER], emitted.at[0, 1]),
        out(2, stage.at[0], grads_out.at[0, 1]),
        out(3, stage.at[1], rebuilt.at[0, 1]),
        out(4, stage.at[2], emitted.at[0, 0]),
        out(5, stage.at[3], grads_out.at[0, 0]),
        out(6, wg, weight_grad.at[0]),
    ]

    along_z(BACK_LOWER).wait_recv()
    along_z(GRAD_UPPER).start()
    along_z(OUT_UPPER).start()
    deal(BACK_LOWER, 0, False)
    outs[0].start()
    gather(0)
    w_copy.wait()
    multiply(0, True)

    along_z(OUT_UPPER).wait_recv()
    deal(OUT_UPPER, 1, False)
    outs[1].start()

    along_z(GRAD_UPPER).wait_recv()
    along_z(BACK_UPPER).start()
    along_z(OUT_LOWER).start()
    along_z(GRAD_LOWER).start()
    for k in range(1, n_d):
        partial(0, k).wait_recv()
    live = lengths[0, 0]

    def keep(block):
        place = lax.broadcasted_iota(jnp.int32, block.shape, 0)
        return jnp.where(place < live, block.astype(f32), 0.0)

    def hide(cols):
        pre = total(0, cols)
        dupper = keep(got[GRAD_UPPER, :, cols])
        stage[0, :, cols] = dupper.astype(bf16)
        sigma = jax.nn.sigmoid(pre)
        gated = (dupper * (sigma * (1.0 + pre * (1.0 - sigma)))).astype(bf16)
        hidden[me_d, :, :, cols] = gated.reshape(n_t, half, 256)

    tiles(hide)

    side = lax.rem(me_d, 2)
    x_near = me_d + 1 - 2 * side
    y_near = lax.rem(me_d + 2, n_d)
    far = lax.rem(x_near + 2, n_d)

    def show(n):
        r, h, target = (
            (me_d, 0, x_near), (me_d, 1, y_near), (me_d, 1, x_near),
            (me_d, 0, y_near), (x_near, 0, y_near), (y_near, 1, x_near),
        )[n]
        block = hidden.at[r, h]
        return remote(block, block, h_send.at[n], h_recv.at[n], (me_s, target, me_t))

    def shown(n):
        r, h = ((x_near, 0), (y_near, 1), (x_near, 1), (y_near, 0), (far, 0), (far, 1))[n]
        landed(hidden.at[r, h], h_recv.at[n])

    for n in range(4):
        show(n).start()
    gather(1)
    multiply(1, False)
    for n in range(2):
        shown(n)
        show(n + 4).start()
    for k in range(1, n_d):
        partial(1, k).start()
    outs[2].start()

    along_z(BACK_UPPER).wait_recv()

    def rebuild(cols):
        pre = total(0, cols)
        upper = got[BACK_UPPER, :, cols].astype(f32)
        stage[1, :, cols] = (upper - pre * jax.nn.sigmoid(pre)).astype(bf16)

    tiles(rebuild)
    outs[3].start()

    for n in range(2, 6):
        shown(n)

    @pl.loop(0, depth // 256)
    def _(c):
        cols = pl.ds(pl.multiple_of(c * 256, 256), 256)
        left = hidden[...].reshape(n_d * rows, local_features)
        product = lax.dot_general(left, w[cols, :], (((1,), (1,)), ((), ())), preferred_element_type=f32)
        terms[:, :, :, cols] = product.reshape(n_d, n_t, half, 256)

    for r in range(n_d):
        tx[r] = terms[r, other].astype(bf16)
    swap = remote(tx, trx, t_send, t_recv, (me_s, me_d, other))
    swap.start()

    def weigh(lo, hi):
        @pl.loop(lo, hi)
        def _(c):
            cols = pl.ds(pl.multiple_of(c * 256, 256), 256)
            left = share[0, :, :, :, cols].reshape(n_d * rows, 256)
            right = hidden[...].reshape(n_d * rows, local_features)
            product = lax.dot_general(left, right, (((0,), (0,)), ((), ())), preferred_element_type=f32)
            wg[cols, :] = product.astype(bf16)

    swap.wait_recv()
    owner, place = lax.div(me_d, per), lax.rem(me_d, per)

    def back_to(k, finish):
        r = replica(k)
        src, dst = ts.at[r], tr.at[place, me_t]
        own = jnp.logical_and(k == 0, me_t == owner)

        @pl.when(own)
        def _():
            if not finish:
                pltpu.make_async_copy(src, dst, f_recv.at[place, me_t]).start()

        @pl.when(jnp.logical_not(own))
        def _():
            copy = remote(src, dst, f_send.at[k], f_recv.at[place, me_t], (me_s, r, owner))
            if finish:
                copy.wait_send()
            else:
                copy.start()

    for k in range(1, n_d + 1):
        r = replica(k)
        ts[r] = (terms[r, me_t] + trx[r].astype(f32)).astype(bf16)
        back_to(k % n_d, False)

    weigh(0, depth // 256)
    outs[6].start()

    along_z(OUT_LOWER).wait_recv()
    for k in range(1, n_d):
        partial(1, k).wait_recv()

    def emit(cols):
        pre = total(1, cols)
        lower = got[OUT_LOWER, :, cols].astype(f32)
        stage[2, :, cols] = (lower + pre * jax.nn.sigmoid(pre)).astype(bf16)

    tiles(emit)
    outs[4].start()

    along_z(GRAD_LOWER).wait_recv()
    for j in range(per):
        for h in range(n_t):
            landed(tr.at[j, h], f_recv.at[j, h])

    for j in range(per):
        span = pl.ds(j * depth, depth)
        through = tr[j].reshape(rows, depth).astype(f32)
        stage[3, :, span] = (keep(got[GRAD_LOWER, :, span]) + through).astype(bf16)
    outs[5].start()

    for i in range(6):
        along_z(i).wait_send()
    for x, i in ((0, BACK_LOWER), (1, OUT_UPPER)):
        deal(i, x, True)
        for k in range(n_d):
            relay(x, k).wait_send()
        for k in range(1, n_d):
            partial(x, k).wait_send()
    for n in range(6):
        show(n).wait_send()
    swap.wait_send()
    for k in range(n_d):
        back_to(k, True)
    for copy in outs:
        copy.wait()


def together(sizes, sent_out, sent_back, sent_grad, lengths, weight):
    n_d, n_t = sizes
    rows, features = sent_out.shape[2:]
    depth = weight.shape[1]
    half, per = rows // n_t, features // depth
    bf16 = jnp.bfloat16
    dma, vmem = pltpu.SemaphoreType.DMA, pltpu.VMEM
    anywhere = pl.BlockSpec(memory_space=pl.ANY)
    return pl.pallas_call(
        step_kernel,
        out_shape=[jax.ShapeDtypeStruct(a.shape, bf16) for a in (sent_out, sent_back, sent_grad, weight)],
        in_specs=[pl.BlockSpec(memory_space=pltpu.SMEM)] + [anywhere] * 4,
        out_specs=[anywhere] * 4,
        scratch_shapes=[
            vmem((depth, features), bf16),
            vmem((6, rows, features), bf16),
            vmem((2, n_d, n_t, half, depth), bf16),
            vmem((2, n_d, rows, features), bf16),
            vmem((2, n_d - 1, rows, features), bf16),
            vmem((n_d, n_t, half, features), bf16),
            vmem((n_d, n_t, half, depth), jnp.float32),
            vmem((n_d, half, depth), bf16),
            vmem((n_d, half, depth), bf16),
            vmem((n_d, half, depth), bf16),
            vmem((per, n_t, half, depth), bf16),
            vmem((4, rows, features), bf16),
            vmem((depth, features), bf16),
            dma((6,)), dma((6,)),
            dma((2, n_t * per)), dma((2, n_d)),
            dma((2, n_d)), dma((2, n_d)),
            dma((2, n_d - 1)), dma((2, n_d - 1)),
            dma((6,)), dma((6,)),
            dma(()), dma(()),
            dma((n_d,)), dma((per, n_t)),
            dma(()), dma((7,)),
        ],
        compiler_params=pltpu.CompilerParams(
            collective_id=0, has_side_effects=True, vmem_limit_bytes=62 * 2**20
        ),
    )(lengths, sent_out, sent_back, sent_grad, weight)


def local(sizes, sent_out, sent_back, sent_grad, lengths, weight):
    n_s, n_d, n_t = sizes
    rows, features = sent_out.shape[2:]
    depth = weight.shape[1]
    fits = n_s > 2 and n_d == 4 and n_t == 2 and rows % 32 == 0 and features % depth == 0 and depth % 256 == 0
    if fits and features % 512 == 0:
        return tuple(together((n_d, n_t), sent_out, sent_back, sent_grad, lengths, weight))
    return spread(sent_out, sent_back, sent_grad, lengths, weight)


def solution(mesh):
    return jax.shard_map(
        functools.partial(local, tuple(mesh.shape[a] for a in ("section", "dp", "tensor"))),
        mesh=mesh,
        in_specs=(
            P("section", None, "dp", "tensor"),
            P("section", None, "dp", "tensor"),
            P("section", None, "dp", "tensor"),
            P("section", "dp"),
            P("section", "dp", "tensor"),
        ),
        out_specs=(
            P("section", None, "dp", "tensor"),
            P("section", None, "dp", "tensor"),
            P("section", None, "dp", "tensor"),
            P("section", "dp", "tensor"),
        ),
        check_vma=False,
    )
```

```python
import functools

import jax
import jax.numpy as jnp
from jax import lax
from jax.experimental import pallas as pl
from jax.experimental.pallas import tpu as pltpu
from jax.sharding import PartitionSpec as P


def shifted(block, axis, distance):
    devices = range(lax.axis_size(axis))
    route = [((i - distance) % len(devices), i) for i in devices]
    return lax.ppermute(block, axis, route)


def across_rows(left, right):
    return lax.dot_general(
        left, right, (((0,), (0,)), ((), ())), preferred_element_type=jnp.float32
    )


def slope(hidden):
    sigma = jax.nn.sigmoid(hidden)
    return sigma * (1.0 + hidden * (1.0 - sigma))


def spread(sent_out, sent_back, sent_grad, lengths, weight):
    token_rows = sent_out.shape[2]
    own_weight = weight[0]

    def shares(block):
        full = lax.all_gather(block, "tensor", axis=1, tiled=True)
        return lax.all_to_all(full, "dp", split_axis=1, concat_axis=0, tiled=True)

    def project(share):
        partial = jnp.dot(share, own_weight, preferred_element_type=jnp.float32)
        return lax.psum_scatter(
            partial.astype(jnp.bfloat16), "dp", scatter_dimension=0, tiled=True
        ).astype(jnp.float32)

    back_lower = shifted(sent_back[0, 1], "section", -1)
    upper_in = shifted(sent_out[0, 0], "section", 1)
    incoming_upper = shifted(sent_grad[0, 0], "section", -1)
    lower_in = shifted(sent_out[0, 1], "section", 1)
    back_upper = shifted(sent_back[0, 0], "section", -1)
    incoming_lower = shifted(sent_grad[0, 1], "section", -1)

    held_share = shares(back_lower)
    pre_held = project(held_share)
    keep = (jnp.arange(token_rows, dtype=jnp.int32) < lengths[0, 0])[:, None]
    zero = jnp.zeros((), jnp.bfloat16)
    dupper = jnp.where(keep, incoming_upper, zero)
    dlower = jnp.where(keep, incoming_lower, zero)
    hidden = (dupper.astype(jnp.float32) * slope(pre_held)).astype(jnp.bfloat16)
    hidden_all = lax.all_gather(hidden, "dp", axis=0, tiled=True)
    rebuilt_lower = (back_upper.astype(jnp.float32) - jax.nn.silu(pre_held)).astype(jnp.bfloat16)
    rebuilt = jnp.stack([back_lower, rebuilt_lower])[None]

    pre = project(shares(upper_in))
    upper_out = (lower_in.astype(jnp.float32) + jax.nn.silu(pre)).astype(jnp.bfloat16)
    emitted = jnp.stack([upper_out, upper_in])[None]

    terms = lax.dot_general(
        hidden_all, own_weight, (((1,), (1,)), ((), ())), preferred_element_type=jnp.float32
    ).astype(jnp.bfloat16)
    terms = lax.all_to_all(terms, "dp", split_axis=0, concat_axis=1, tiled=True)
    through = lax.psum_scatter(terms, "tensor", scatter_dimension=1, tiled=True).astype(jnp.float32)
    dupper_in = (dlower.astype(jnp.float32) + through).astype(jnp.bfloat16)
    grads_out = jnp.stack([dupper_in, dupper])[None]
    weight_grad = across_rows(held_share, hidden_all).astype(jnp.bfloat16)[None]
    return (emitted, rebuilt, grads_out, weight_grad)


MESH = pl.DeviceIdType.MESH
BACK_LOWER, GRAD_UPPER, BACK_UPPER, GRAD_LOWER, OUT_UPPER, OUT_LOWER = range(6)


def step_kernel(
    lengths, sent_out, sent_back, sent_grad, weight,
    emitted, rebuilt, grads_out, weight_grad,
    w, got, share, part, summed, hidden, terms, tx, trx, ts, tr, stage, wg,
    z_send, z_recv, b_send, b_recv, d_send, d_recv, r_send, r_recv, p_send, p_recv,
    h_send, h_recv, t_send, t_recv, f_send, f_recv, w_sem, o_sem,
):
    f32, bf16 = jnp.float32, jnp.bfloat16
    n_s, n_d, n_t = (lax.axis_size(a) for a in ("section", "dp", "tensor"))
    me_s, me_d, me_t = (lax.axis_index(a) for a in ("section", "dp", "tensor"))
    rows, local_features = got.shape[1], got.shape[2]
    half, depth = share.shape[3], share.shape[4]
    per = local_features // depth
    other = 1 - me_t
    nxt, prv = lax.rem(me_s + 1, n_s), lax.rem(me_s + n_s - 1, n_s)

    def replica(k):
        return lax.rem(me_d + k + n_d, n_d)

    side = lax.rem(me_d, 2)
    x_near = me_d + 1 - 2 * side
    y_near = lax.rem(me_d + 2, n_d)
    far = lax.rem(x_near + 2, n_d)

    barrier = pltpu.get_barrier_semaphore()
    for k in range(n_d):
        for c in range(n_t):
            if k or c:
                pl.semaphore_signal(
                    barrier, inc=1, device_id=(me_s, replica(k), lax.rem(me_t + c, n_t)), device_id_type=MESH
                )
    for z in (nxt, prv):
        pl.semaphore_signal(barrier, inc=1, device_id=(z, me_d, me_t), device_id_type=MESH)
    pl.semaphore_wait(barrier, n_d * n_t - 1 + 2)

    def remote(src, dst, send, recv, where):
        return pltpu.make_async_remote_copy(
            src_ref=src, dst_ref=dst, send_sem=send, recv_sem=recv, device_id=where, device_id_type=MESH
        )

    def landed(dst, sem):
        pltpu.make_async_copy(dst, dst, sem).wait()

    def along_z(i):
        src, piece, z = {
            BACK_LOWER: (sent_back, 1, prv), BACK_UPPER: (sent_back, 0, prv),
            GRAD_UPPER: (sent_grad, 0, prv), GRAD_LOWER: (sent_grad, 1, prv),
            OUT_UPPER: (sent_out, 0, nxt), OUT_LOWER: (sent_out, 1, nxt),
        }[i]
        return remote(src.at[0, piece], got.at[i], z_send.at[i], z_recv.at[i], (z, me_d, me_t))

    def back_lower(n):
        h, j = n // per, n % per
        piece = (pl.ds(h * half, half), pl.ds(j * depth, depth))
        return remote(
            sent_back.at[0, 1, *piece], got.at[BACK_LOWER, *piece], b_send.at[n], b_recv.at[n], (prv, me_d, me_t)
        )

    for n in range(n_t * per):
        back_lower(n).start()
    w_copy = pltpu.make_async_copy(weight.at[0], w, w_sem)
    w_copy.start()

    def deal(i, x, finish):
        for h in range(n_t):
            for j in range(per):
                n = h * per + j
                if i == BACK_LOWER and not finish:
                    back_lower(n).wait_recv()
                target = me_t * per + j
                src = got.at[i, pl.ds(h * half, half), pl.ds(j * depth, depth)]
                dst = share.at[x, me_d, h]
                own = jnp.logical_and(target == me_d, me_t == h)

                @pl.when(own)
                def _():
                    if not finish:
                        pltpu.make_async_copy(src, dst, d_recv.at[x, me_d]).start()

                @pl.when(jnp.logical_not(own))
                def _():
                    copy = remote(src, dst, d_send.at[x, n], d_recv.at[x, me_d], (me_s, target, h))
                    if finish:
                        copy.wait_send()
                    else:
                        copy.start()

    def relay(x, k):
        r = replica(k)
        return remote(
            share.at[x, r, me_t], share.at[x, r, me_t], r_send.at[x, r], r_recv.at[x, r], (me_s, me_d, other)
        )

    wide = local_features // 2

    def partial(x, n):
        r, side_of, target = (
            (far, 0, x_near), (far, 1, y_near), (x_near, 0, x_near),
            (y_near, 1, y_near), (y_near, 0, y_near), (x_near, 1, x_near),
        )[n]
        return remote(
            part.at[x, r, :, pl.ds(side_of * wide, wide)], summed.at[x, n],
            p_send.at[x, n], p_recv.at[x, n], (me_s, target, me_t),
        )

    def combine(x):
        for n in range(2):
            r = (y_near, x_near)[n]
            partial(x, n).wait_recv()
            for c in range(wide // 256):
                near = pl.ds(c * 256, 256)
                cols = pl.ds(n * wide + c * 256, 256)
                both = part[x, r, :, cols].astype(f32) + summed[x, n, :, near].astype(f32)
                part[x, r, :, cols] = both.astype(bf16)
            partial(x, n + 4).start()

    def gather(x):
        for k in range(n_d):
            landed(share.at[x, replica(k), me_t], d_recv.at[x, replica(k)])
            relay(x, k).start()
        for k in range(n_d):
            landed(share.at[x, replica(k), other], r_recv.at[x, replica(k)])

    def multiply(x, send):
        for k, r in enumerate((far, x_near, y_near, me_d)):

            @pl.loop(0, local_features // 512)
            def _(c):
                cols = pl.ds(pl.multiple_of(c * 512, 512), 512)
                left = share[x, r].reshape(rows, depth)
                part[x, r, :, cols] = jnp.dot(left, w[:, cols], preferred_element_type=f32).astype(bf16)

            if send:
                for n in ((0, 1), (2,), (3,), ())[k]:
                    partial(x, n).start()

    def total(x, c):
        cols = pl.ds(pl.multiple_of(c * 256, 256), 256)
        n = lax.div(c, wide // 256)
        near = pl.ds(pl.multiple_of(lax.rem(c, wide // 256) * 256, 256), 256)
        pre = part[x, me_d, :, cols].astype(f32)
        return pre + summed[x, 2 + n, :, near].astype(f32) + summed[x, 4 + n, :, near].astype(f32)

    def tiles(body):
        @pl.loop(0, local_features // 256)
        def _(c):
            body(c, pl.ds(pl.multiple_of(c * 256, 256), 256))

    def out(i, src, dst):
        return pltpu.make_async_copy(src, dst, o_sem.at[i])

    outs = [
        out(0, got.at[BACK_LOWER], rebuilt.at[0, 0]),
        out(1, got.at[OUT_UPPER], emitted.at[0, 1]),
        out(2, stage.at[0], grads_out.at[0, 1]),
        out(3, stage.at[1], rebuilt.at[0, 1]),
        out(4, stage.at[2], emitted.at[0, 0]),
        out(5, stage.at[3], grads_out.at[0, 0]),
        out(6, wg, weight_grad.at[0]),
    ]

    deal(BACK_LOWER, 0, False)
    along_z(GRAD_UPPER).start()
    along_z(OUT_UPPER).start()
    outs[0].start()
    gather(0)
    w_copy.wait()
    multiply(0, True)
    combine(0)

    along_z(OUT_UPPER).wait_recv()
    deal(OUT_UPPER, 1, False)
    outs[1].start()

    along_z(GRAD_UPPER).wait_recv()
    along_z(BACK_UPPER).start()
    along_z(OUT_LOWER).start()
    along_z(GRAD_LOWER).start()
    for n in range(2, 6):
        partial(0, n).wait_recv()
    live = lengths[0, 0]

    def keep(block):
        place = lax.broadcasted_iota(jnp.int32, block.shape, 0)
        return jnp.where(place < live, block.astype(f32), 0.0)

    def hide(c, cols):
        pre = total(0, c)
        dupper = keep(got[GRAD_UPPER, :, cols])
        stage[0, :, cols] = dupper.astype(bf16)
        sigma = jax.nn.sigmoid(pre)
        gated = (dupper * (sigma * (1.0 + pre * (1.0 - sigma)))).astype(bf16)
        hidden[me_d, :, :, cols] = gated.reshape(n_t, half, 256)

    tiles(hide)

    def show(n):
        r, h, target = (
            (me_d, 0, x_near), (me_d, 1, y_near), (me_d, 1, x_near),
            (me_d, 0, y_near), (x_near, 0, y_near), (y_near, 1, x_near),
        )[n]
        block = hidden.at[r, h]
        return remote(block, block, h_send.at[n], h_recv.at[n], (me_s, target, me_t))

    def shown(n):
        r, h = ((x_near, 0), (y_near, 1), (x_near, 1), (y_near, 0), (far, 0), (far, 1))[n]
        landed(hidden.at[r, h], h_recv.at[n])

    for n in range(4):
        show(n).start()
    gather(1)
    multiply(1, False)
    for n in range(2):
        shown(n)
        show(n + 4).start()
    for n in range(4):
        partial(1, n).start()
    outs[2].start()

    along_z(BACK_UPPER).wait_recv()

    def rebuild(c, cols):
        pre = total(0, c)
        upper = got[BACK_UPPER, :, cols].astype(f32)
        stage[1, :, cols] = (upper - pre * jax.nn.sigmoid(pre)).astype(bf16)

    tiles(rebuild)
    outs[3].start()

    for n in range(2, 6):
        shown(n)

    @pl.loop(0, depth // 256)
    def _(c):
        cols = pl.ds(pl.multiple_of(c * 256, 256), 256)
        left = hidden[...].reshape(n_d * rows, local_features)
        product = lax.dot_general(left, w[cols, :], (((1,), (1,)), ((), ())), preferred_element_type=f32)
        terms[:, :, :, cols] = product.reshape(n_d, n_t, half, 256)

    for r in range(n_d):
        tx[r] = terms[r, other].astype(bf16)
    swap = remote(tx, trx, t_send, t_recv, (me_s, me_d, other))
    swap.start()
    combine(1)

    def weigh(lo, hi):
        @pl.loop(lo, hi)
        def _(c):
            cols = pl.ds(pl.multiple_of(c * 256, 256), 256)
            left = share[0, :, :, :, cols].reshape(n_d * rows, 256)
            right = hidden[...].reshape(n_d * rows, local_features)
            product = lax.dot_general(left, right, (((0,), (0,)), ((), ())), preferred_element_type=f32)
            wg[cols, :] = product.astype(bf16)

    swap.wait_recv()
    owner, place = lax.div(me_d, per), lax.rem(me_d, per)

    def back_to(k, finish):
        r = replica(k)
        src, dst = ts.at[r], tr.at[place, me_t]
        own = jnp.logical_and(k == 0, me_t == owner)

        @pl.when(own)
        def _():
            if not finish:
                pltpu.make_async_copy(src, dst, f_recv.at[place, me_t]).start()

        @pl.when(jnp.logical_not(own))
        def _():
            copy = remote(src, dst, f_send.at[k], f_recv.at[place, me_t], (me_s, r, owner))
            if finish:
                copy.wait_send()
            else:
                copy.start()

    for k in range(1, n_d + 1):
        r = replica(k)
        ts[r] = (terms[r, me_t] + trx[r].astype(f32)).astype(bf16)
        back_to(k % n_d, False)

    weigh(0, depth // 256)
    outs[6].start()

    along_z(OUT_LOWER).wait_recv()
    for n in range(2, 6):
        partial(1, n).wait_recv()

    def emit(c, cols):
        pre = total(1, c)
        lower = got[OUT_LOWER, :, cols].astype(f32)
        stage[2, :, cols] = (lower + pre * jax.nn.sigmoid(pre)).astype(bf16)

    tiles(emit)
    outs[4].start()

    along_z(GRAD_LOWER).wait_recv()
    for j in range(per):
        for h in range(n_t):
            landed(tr.at[j, h], f_recv.at[j, h])

    for j in range(per):
        span = pl.ds(j * depth, depth)
        through = tr[j].reshape(rows, depth).astype(f32)
        stage[3, :, span] = (keep(got[GRAD_LOWER, :, span]) + through).astype(bf16)
    outs[5].start()

    for n in range(n_t * per):
        back_lower(n).wait_send()
    for i in range(1, 6):
        along_z(i).wait_send()
    for x, i in ((0, BACK_LOWER), (1, OUT_UPPER)):
        deal(i, x, True)
        for k in range(n_d):
            relay(x, k).wait_send()
        for n in range(6):
            partial(x, n).wait_send()
    for n in range(6):
        show(n).wait_send()
    swap.wait_send()
    for k in range(n_d):
        back_to(k, True)
    for copy in outs:
        copy.wait()


def together(sizes, sent_out, sent_back, sent_grad, lengths, weight):
    n_d, n_t = sizes
    rows, features = sent_out.shape[2:]
    depth = weight.shape[1]
    half, per = rows // n_t, features // depth
    bf16 = jnp.bfloat16
    dma, vmem = pltpu.SemaphoreType.DMA, pltpu.VMEM
    anywhere = pl.BlockSpec(memory_space=pl.ANY)
    return pl.pallas_call(
        step_kernel,
        out_shape=[jax.ShapeDtypeStruct(a.shape, bf16) for a in (sent_out, sent_back, sent_grad, weight)],
        in_specs=[pl.BlockSpec(memory_space=pltpu.SMEM)] + [anywhere] * 4,
        out_specs=[anywhere] * 4,
        scratch_shapes=[
            vmem((depth, features), bf16),
            vmem((6, rows, features), bf16),
            vmem((2, n_d, n_t, half, depth), bf16),
            vmem((2, n_d, rows, features), bf16),
            vmem((2, 6, rows, features // 2), bf16),
            vmem((n_d, n_t, half, features), bf16),
            vmem((n_d, n_t, half, depth), jnp.float32),
            vmem((n_d, half, depth), bf16),
            vmem((n_d, half, depth), bf16),
            vmem((n_d, half, depth), bf16),
            vmem((per, n_t, half, depth), bf16),
            vmem((4, rows, features), bf16),
            vmem((depth, features), bf16),
            dma((6,)), dma((6,)),
            dma((n_t * per,)), dma((n_t * per,)),
            dma((2, n_t * per)), dma((2, n_d)),
            dma((2, n_d)), dma((2, n_d)),
            dma((2, 6)), dma((2, 6)),
            dma((6,)), dma((6,)),
            dma(()), dma(()),
            dma((n_d,)), dma((per, n_t)),
            dma(()), dma((7,)),
        ],
        compiler_params=pltpu.CompilerParams(
            collective_id=0, has_side_effects=True, vmem_limit_bytes=62 * 2**20
        ),
    )(lengths, sent_out, sent_back, sent_grad, weight)


def local(sizes, sent_out, sent_back, sent_grad, lengths, weight):
    n_s, n_d, n_t = sizes
    rows, features = sent_out.shape[2:]
    depth = weight.shape[1]
    fits = n_s > 2 and n_d == 4 and n_t == 2 and rows % 32 == 0 and features % depth == 0 and depth % 256 == 0
    if fits and features % 512 == 0:
        return tuple(together((n_d, n_t), sent_out, sent_back, sent_grad, lengths, weight))
    return spread(sent_out, sent_back, sent_grad, lengths, weight)


def solution(mesh):
    return jax.shard_map(
        functools.partial(local, tuple(mesh.shape[a] for a in ("section", "dp", "tensor"))),
        mesh=mesh,
        in_specs=(
            P("section", None, "dp", "tensor"),
            P("section", None, "dp", "tensor"),
            P("section", None, "dp", "tensor"),
            P("section", "dp"),
            P("section", "dp", "tensor"),
        ),
        out_specs=(
            P("section", None, "dp", "tensor"),
            P("section", None, "dp", "tensor"),
            P("section", None, "dp", "tensor"),
            P("section", "dp", "tensor"),
        ),
        check_vma=False,
    )
```

```python
import functools

import jax
import jax.numpy as jnp
from jax import lax
from jax.experimental import pallas as pl
from jax.experimental.pallas import tpu as pltpu
from jax.sharding import PartitionSpec as P


def shifted(block, axis, distance):
    devices = range(lax.axis_size(axis))
    route = [((i - distance) % len(devices), i) for i in devices]
    return lax.ppermute(block, axis, route)


def across_rows(left, right):
    return lax.dot_general(
        left, right, (((0,), (0,)), ((), ())), preferred_element_type=jnp.float32
    )


def slope(hidden):
    sigma = jax.nn.sigmoid(hidden)
    return sigma * (1.0 + hidden * (1.0 - sigma))


def spread(sent_out, sent_back, sent_grad, lengths, weight):
    token_rows = sent_out.shape[2]
    own_weight = weight[0]

    def shares(block):
        full = lax.all_gather(block, "tensor", axis=1, tiled=True)
        return lax.all_to_all(full, "dp", split_axis=1, concat_axis=0, tiled=True)

    def project(share):
        partial = jnp.dot(share, own_weight, preferred_element_type=jnp.float32)
        return lax.psum_scatter(
            partial.astype(jnp.bfloat16), "dp", scatter_dimension=0, tiled=True
        ).astype(jnp.float32)

    back_lower = shifted(sent_back[0, 1], "section", -1)
    upper_in = shifted(sent_out[0, 0], "section", 1)
    incoming_upper = shifted(sent_grad[0, 0], "section", -1)
    lower_in = shifted(sent_out[0, 1], "section", 1)
    back_upper = shifted(sent_back[0, 0], "section", -1)
    incoming_lower = shifted(sent_grad[0, 1], "section", -1)

    held_share = shares(back_lower)
    pre_held = project(held_share)
    keep = (jnp.arange(token_rows, dtype=jnp.int32) < lengths[0, 0])[:, None]
    zero = jnp.zeros((), jnp.bfloat16)
    dupper = jnp.where(keep, incoming_upper, zero)
    dlower = jnp.where(keep, incoming_lower, zero)
    hidden = (dupper.astype(jnp.float32) * slope(pre_held)).astype(jnp.bfloat16)
    hidden_all = lax.all_gather(hidden, "dp", axis=0, tiled=True)
    rebuilt_lower = (back_upper.astype(jnp.float32) - jax.nn.silu(pre_held)).astype(jnp.bfloat16)
    rebuilt = jnp.stack([back_lower, rebuilt_lower])[None]

    pre = project(shares(upper_in))
    upper_out = (lower_in.astype(jnp.float32) + jax.nn.silu(pre)).astype(jnp.bfloat16)
    emitted = jnp.stack([upper_out, upper_in])[None]

    terms = lax.dot_general(
        hidden_all, own_weight, (((1,), (1,)), ((), ())), preferred_element_type=jnp.float32
    ).astype(jnp.bfloat16)
    terms = lax.all_to_all(terms, "dp", split_axis=0, concat_axis=1, tiled=True)
    through = lax.psum_scatter(terms, "tensor", scatter_dimension=1, tiled=True).astype(jnp.float32)
    dupper_in = (dlower.astype(jnp.float32) + through).astype(jnp.bfloat16)
    grads_out = jnp.stack([dupper_in, dupper])[None]
    weight_grad = across_rows(held_share, hidden_all).astype(jnp.bfloat16)[None]
    return (emitted, rebuilt, grads_out, weight_grad)


MESH = pl.DeviceIdType.MESH
BACK_LOWER, GRAD_UPPER, BACK_UPPER, GRAD_LOWER, OUT_UPPER, OUT_LOWER = range(6)


def step_kernel(
    lengths, sent_out, sent_back, sent_grad, weight,
    emitted, rebuilt, grads_out, weight_grad,
    w, got, share, part, summed, hidden, terms, tx, trx, ts, tr, stage, wg,
    z_send, z_recv, b_send, b_recv, d_send, d_recv, r_send, r_recv, p_send, p_recv,
    h_send, h_recv, t_send, t_recv, f_send, f_recv, w_sem, o_sem,
):
    f32, bf16 = jnp.float32, jnp.bfloat16
    n_s, n_d, n_t = (lax.axis_size(a) for a in ("section", "dp", "tensor"))
    me_s, me_d, me_t = (lax.axis_index(a) for a in ("section", "dp", "tensor"))
    rows, local_features = got.shape[1], got.shape[2]
    half, depth = share.shape[3], share.shape[4]
    per = local_features // depth
    other = 1 - me_t
    nxt, prv = lax.rem(me_s + 1, n_s), lax.rem(me_s + n_s - 1, n_s)

    def replica(k):
        return lax.rem(me_d + k + n_d, n_d)

    side = lax.rem(me_d, 2)
    x_near = me_d + 1 - 2 * side
    y_near = lax.rem(me_d + 2, n_d)
    far = lax.rem(x_near + 2, n_d)

    barrier = pltpu.get_barrier_semaphore()
    for k in range(n_d):
        for c in range(n_t):
            if k or c:
                pl.semaphore_signal(
                    barrier, inc=1, device_id=(me_s, replica(k), lax.rem(me_t + c, n_t)), device_id_type=MESH
                )
    for z in (nxt, prv):
        pl.semaphore_signal(barrier, inc=1, device_id=(z, me_d, me_t), device_id_type=MESH)
    pl.semaphore_wait(barrier, n_d * n_t - 1 + 2)

    def remote(src, dst, send, recv, where):
        return pltpu.make_async_remote_copy(
            src_ref=src, dst_ref=dst, send_sem=send, recv_sem=recv, device_id=where, device_id_type=MESH
        )

    def landed(dst, sem):
        pltpu.make_async_copy(dst, dst, sem).wait()

    def along_z(i):
        src, piece, z = {
            BACK_LOWER: (sent_back, 1, prv), BACK_UPPER: (sent_back, 0, prv),
            GRAD_UPPER: (sent_grad, 0, prv), GRAD_LOWER: (sent_grad, 1, prv),
            OUT_UPPER: (sent_out, 0, nxt), OUT_LOWER: (sent_out, 1, nxt),
        }[i]
        return remote(src.at[0, piece], got.at[i], z_send.at[i], z_recv.at[i], (z, me_d, me_t))

    def back_lower(n):
        h, j = n // per, n % per
        piece = (pl.ds(h * half, half), pl.ds(j * depth, depth))
        return remote(
            sent_back.at[0, 1, *piece], got.at[BACK_LOWER, *piece], b_send.at[n], b_recv.at[n], (prv, me_d, me_t)
        )

    for n in range(n_t * per):
        back_lower(n).start()
    w_copy = pltpu.make_async_copy(weight.at[0], w, w_sem)
    w_copy.start()

    def deal(i, x, finish):
        for h in range(n_t):
            for j in range(per):
                n = h * per + j
                if i == BACK_LOWER and not finish:
                    back_lower(n).wait_recv()
                target = me_t * per + j
                src = got.at[i, pl.ds(h * half, half), pl.ds(j * depth, depth)]
                dst = share.at[x, me_d, h]
                own = jnp.logical_and(target == me_d, me_t == h)

                @pl.when(own)
                def _():
                    if not finish:
                        pltpu.make_async_copy(src, dst, d_recv.at[x, me_d]).start()

                @pl.when(jnp.logical_not(own))
                def _():
                    copy = remote(src, dst, d_send.at[x, n], d_recv.at[x, me_d], (me_s, target, h))
                    if finish:
                        copy.wait_send()
                    else:
                        copy.start()

    def relay(x, k):
        r = replica(k)
        return remote(
            share.at[x, r, me_t], share.at[x, r, me_t], r_send.at[x, r], r_recv.at[x, r], (me_s, me_d, other)
        )

    wide = local_features // 2

    def partial(x, n):
        r, side_of, target = (
            (far, 0, x_near), (far, 1, y_near), (x_near, 0, x_near),
            (y_near, 1, y_near), (y_near, 0, y_near), (x_near, 1, x_near),
        )[n]
        return remote(
            part.at[x, r, :, pl.ds(side_of * wide, wide)], summed.at[x, n],
            p_send.at[x, n], p_recv.at[x, n], (me_s, target, me_t),
        )

    def combine(x):
        for n in range(2):
            r = (y_near, x_near)[n]
            partial(x, n).wait_recv()
            for c in range(wide // 256):
                near = pl.ds(c * 256, 256)
                cols = pl.ds(n * wide + c * 256, 256)
                both = part[x, r, :, cols].astype(f32) + summed[x, n, :, near].astype(f32)
                part[x, r, :, cols] = both.astype(bf16)
            partial(x, n + 4).start()

    def gather(x):
        for k in range(n_d):
            landed(share.at[x, replica(k), me_t], d_recv.at[x, replica(k)])
            relay(x, k).start()
        for k in range(n_d):
            landed(share.at[x, replica(k), other], r_recv.at[x, replica(k)])

    def multiply(x):
        for k, r in enumerate((far, x_near, y_near, me_d)):

            @pl.loop(0, local_features // 512)
            def _(c):
                cols = pl.ds(pl.multiple_of(c * 512, 512), 512)
                left = share[x, r].reshape(rows, depth)
                part[x, r, :, cols] = jnp.dot(left, w[:, cols], preferred_element_type=f32).astype(bf16)

            for n in ((0, 1), (2,), (3,), ())[k]:
                partial(x, n).start()

    def total(x, c):
        cols = pl.ds(pl.multiple_of(c * 256, 256), 256)
        n = lax.div(c, wide // 256)
        near = pl.ds(pl.multiple_of(lax.rem(c, wide // 256) * 256, 256), 256)
        pre = part[x, me_d, :, cols].astype(f32)
        return pre + summed[x, 2 + n, :, near].astype(f32) + summed[x, 4 + n, :, near].astype(f32)

    def tiles(body):
        @pl.loop(0, local_features // 256)
        def _(c):
            body(c, pl.ds(pl.multiple_of(c * 256, 256), 256))

    def out(i, src, dst):
        return pltpu.make_async_copy(src, dst, o_sem.at[i])

    outs = [
        out(0, got.at[BACK_LOWER], rebuilt.at[0, 0]),
        out(1, got.at[OUT_UPPER], emitted.at[0, 1]),
        out(2, stage.at[0], grads_out.at[0, 1]),
        out(3, stage.at[1], rebuilt.at[0, 1]),
        out(4, stage.at[2], emitted.at[0, 0]),
        out(5, stage.at[3], grads_out.at[0, 0]),
        out(6, wg, weight_grad.at[0]),
    ]

    deal(BACK_LOWER, 0, False)
    along_z(GRAD_UPPER).start()
    outs[0].start()
    gather(0)
    w_copy.wait()
    multiply(0)
    along_z(GRAD_UPPER).wait_recv()
    along_z(OUT_UPPER).start()
    combine(0)
    for n in range(2, 6):
        partial(0, n).wait_recv()
    live = lengths[0, 0]

    def keep(block):
        place = lax.broadcasted_iota(jnp.int32, block.shape, 0)
        return jnp.where(place < live, block.astype(f32), 0.0)

    def hide(c, cols):
        pre = total(0, c)
        dupper = keep(got[GRAD_UPPER, :, cols])
        stage[0, :, cols] = dupper.astype(bf16)
        sigma = jax.nn.sigmoid(pre)
        gated = (dupper * (sigma * (1.0 + pre * (1.0 - sigma)))).astype(bf16)
        hidden[me_d, :, :, cols] = gated.reshape(n_t, half, 256)

    tiles(hide)

    def show(n):
        r, h, target = (
            (me_d, 0, x_near), (me_d, 1, y_near), (me_d, 1, x_near),
            (me_d, 0, y_near), (x_near, 0, y_near), (y_near, 1, x_near),
        )[n]
        block = hidden.at[r, h]
        return remote(block, block, h_send.at[n], h_recv.at[n], (me_s, target, me_t))

    def shown(n):
        r, h = ((x_near, 0), (y_near, 1), (x_near, 1), (y_near, 0), (far, 0), (far, 1))[n]
        landed(hidden.at[r, h], h_recv.at[n])

    for n in range(4):
        show(n).start()
    along_z(OUT_UPPER).wait_recv()
    along_z(BACK_UPPER).start()
    along_z(OUT_LOWER).start()
    along_z(GRAD_LOWER).start()
    deal(OUT_UPPER, 1, False)
    outs[1].start()
    for n in range(2):
        shown(n)
        show(n + 4).start()
    gather(1)
    multiply(1)
    outs[2].start()

    along_z(BACK_UPPER).wait_recv()

    def rebuild(c, cols):
        pre = total(0, c)
        upper = got[BACK_UPPER, :, cols].astype(f32)
        stage[1, :, cols] = (upper - pre * jax.nn.sigmoid(pre)).astype(bf16)

    tiles(rebuild)
    outs[3].start()

    for n in range(2, 6):
        shown(n)

    @pl.loop(0, depth // 256)
    def _(c):
        cols = pl.ds(pl.multiple_of(c * 256, 256), 256)
        left = hidden[...].reshape(n_d * rows, local_features)
        product = lax.dot_general(left, w[cols, :], (((1,), (1,)), ((), ())), preferred_element_type=f32)
        terms[:, :, :, cols] = product.reshape(n_d, n_t, half, 256)

    for r in range(n_d):
        tx[r] = terms[r, other].astype(bf16)
    swap = remote(tx, trx, t_send, t_recv, (me_s, me_d, other))
    swap.start()
    combine(1)

    def weigh(lo, hi):
        @pl.loop(lo, hi)
        def _(c):
            cols = pl.ds(pl.multiple_of(c * 256, 256), 256)
            left = share[0, :, :, :, cols].reshape(n_d * rows, 256)
            right = hidden[...].reshape(n_d * rows, local_features)
            product = lax.dot_general(left, right, (((0,), (0,)), ((), ())), preferred_element_type=f32)
            wg[cols, :] = product.astype(bf16)

    swap.wait_recv()
    owner, place = lax.div(me_d, per), lax.rem(me_d, per)

    def back_to(k, finish):
        r = replica(k)
        src, dst = ts.at[r], tr.at[place, me_t]
        own = jnp.logical_and(k == 0, me_t == owner)

        @pl.when(own)
        def _():
            if not finish:
                pltpu.make_async_copy(src, dst, f_recv.at[place, me_t]).start()

        @pl.when(jnp.logical_not(own))
        def _():
            copy = remote(src, dst, f_send.at[k], f_recv.at[place, me_t], (me_s, r, owner))
            if finish:
                copy.wait_send()
            else:
                copy.start()

    for k in range(1, n_d + 1):
        r = replica(k)
        ts[r] = (terms[r, me_t] + trx[r].astype(f32)).astype(bf16)
        back_to(k % n_d, False)

    weigh(0, depth // 256)
    outs[6].start()

    along_z(OUT_LOWER).wait_recv()
    for n in range(2, 6):
        partial(1, n).wait_recv()

    def emit(c, cols):
        pre = total(1, c)
        lower = got[OUT_LOWER, :, cols].astype(f32)
        stage[2, :, cols] = (lower + pre * jax.nn.sigmoid(pre)).astype(bf16)

    tiles(emit)
    outs[4].start()

    along_z(GRAD_LOWER).wait_recv()
    for j in range(per):
        for h in range(n_t):
            landed(tr.at[j, h], f_recv.at[j, h])

    for j in range(per):
        span = pl.ds(j * depth, depth)
        through = tr[j].reshape(rows, depth).astype(f32)
        stage[3, :, span] = (keep(got[GRAD_LOWER, :, span]) + through).astype(bf16)
    outs[5].start()

    for n in range(n_t * per):
        back_lower(n).wait_send()
    for i in range(1, 6):
        along_z(i).wait_send()
    for x, i in ((0, BACK_LOWER), (1, OUT_UPPER)):
        deal(i, x, True)
        for k in range(n_d):
            relay(x, k).wait_send()
        for n in range(6):
            partial(x, n).wait_send()
    for n in range(6):
        show(n).wait_send()
    swap.wait_send()
    for k in range(n_d):
        back_to(k, True)
    for copy in outs:
        copy.wait()


def together(sizes, sent_out, sent_back, sent_grad, lengths, weight):
    n_d, n_t = sizes
    rows, features = sent_out.shape[2:]
    depth = weight.shape[1]
    half, per = rows // n_t, features // depth
    bf16 = jnp.bfloat16
    dma, vmem = pltpu.SemaphoreType.DMA, pltpu.VMEM
    anywhere = pl.BlockSpec(memory_space=pl.ANY)
    return pl.pallas_call(
        step_kernel,
        out_shape=[jax.ShapeDtypeStruct(a.shape, bf16) for a in (sent_out, sent_back, sent_grad, weight)],
        in_specs=[pl.BlockSpec(memory_space=pltpu.SMEM)] + [anywhere] * 4,
        out_specs=[anywhere] * 4,
        scratch_shapes=[
            vmem((depth, features), bf16),
            vmem((6, rows, features), bf16),
            vmem((2, n_d, n_t, half, depth), bf16),
            vmem((2, n_d, rows, features), bf16),
            vmem((2, 6, rows, features // 2), bf16),
            vmem((n_d, n_t, half, features), bf16),
            vmem((n_d, n_t, half, depth), jnp.float32),
            vmem((n_d, half, depth), bf16),
            vmem((n_d, half, depth), bf16),
            vmem((n_d, half, depth), bf16),
            vmem((per, n_t, half, depth), bf16),
            vmem((4, rows, features), bf16),
            vmem((depth, features), bf16),
            dma((6,)), dma((6,)),
            dma((n_t * per,)), dma((n_t * per,)),
            dma((2, n_t * per)), dma((2, n_d)),
            dma((2, n_d)), dma((2, n_d)),
            dma((2, 6)), dma((2, 6)),
            dma((6,)), dma((6,)),
            dma(()), dma(()),
            dma((n_d,)), dma((per, n_t)),
            dma(()), dma((7,)),
        ],
        compiler_params=pltpu.CompilerParams(
            collective_id=0, has_side_effects=True, vmem_limit_bytes=62 * 2**20
        ),
    )(lengths, sent_out, sent_back, sent_grad, weight)


def local(sizes, sent_out, sent_back, sent_grad, lengths, weight):
    n_s, n_d, n_t = sizes
    rows, features = sent_out.shape[2:]
    depth = weight.shape[1]
    fits = n_s > 2 and n_d == 4 and n_t == 2 and rows % 32 == 0 and features % depth == 0 and depth % 256 == 0
    if fits and features % 512 == 0:
        return tuple(together((n_d, n_t), sent_out, sent_back, sent_grad, lengths, weight))
    return spread(sent_out, sent_back, sent_grad, lengths, weight)


def solution(mesh):
    return jax.shard_map(
        functools.partial(local, tuple(mesh.shape[a] for a in ("section", "dp", "tensor"))),
        mesh=mesh,
        in_specs=(
            P("section", None, "dp", "tensor"),
            P("section", None, "dp", "tensor"),
            P("section", None, "dp", "tensor"),
            P("section", "dp"),
            P("section", "dp", "tensor"),
        ),
        out_specs=(
            P("section", None, "dp", "tensor"),
            P("section", None, "dp", "tensor"),
            P("section", None, "dp", "tensor"),
            P("section", "dp", "tensor"),
        ),
        check_vma=False,
    )
```

```python
import functools

import jax
import jax.numpy as jnp
from jax import lax
from jax.experimental import pallas as pl
from jax.experimental.pallas import tpu as pltpu
from jax.sharding import PartitionSpec as P


def shifted(block, axis, distance):
    devices = range(lax.axis_size(axis))
    route = [((i - distance) % len(devices), i) for i in devices]
    return lax.ppermute(block, axis, route)


def across_rows(left, right):
    return lax.dot_general(
        left, right, (((0,), (0,)), ((), ())), preferred_element_type=jnp.float32
    )


def slope(hidden):
    sigma = jax.nn.sigmoid(hidden)
    return sigma * (1.0 + hidden * (1.0 - sigma))


def spread(sent_out, sent_back, sent_grad, lengths, weight):
    token_rows = sent_out.shape[2]
    own_weight = weight[0]

    def shares(block):
        full = lax.all_gather(block, "tensor", axis=1, tiled=True)
        return lax.all_to_all(full, "dp", split_axis=1, concat_axis=0, tiled=True)

    def project(share):
        partial = jnp.dot(share, own_weight, preferred_element_type=jnp.float32)
        return lax.psum_scatter(
            partial.astype(jnp.bfloat16), "dp", scatter_dimension=0, tiled=True
        ).astype(jnp.float32)

    back_lower = shifted(sent_back[0, 1], "section", -1)
    upper_in = shifted(sent_out[0, 0], "section", 1)
    incoming_upper = shifted(sent_grad[0, 0], "section", -1)
    lower_in = shifted(sent_out[0, 1], "section", 1)
    back_upper = shifted(sent_back[0, 0], "section", -1)
    incoming_lower = shifted(sent_grad[0, 1], "section", -1)

    held_share = shares(back_lower)
    pre_held = project(held_share)
    keep = (jnp.arange(token_rows, dtype=jnp.int32) < lengths[0, 0])[:, None]
    zero = jnp.zeros((), jnp.bfloat16)
    dupper = jnp.where(keep, incoming_upper, zero)
    dlower = jnp.where(keep, incoming_lower, zero)
    hidden = (dupper.astype(jnp.float32) * slope(pre_held)).astype(jnp.bfloat16)
    hidden_all = lax.all_gather(hidden, "dp", axis=0, tiled=True)
    rebuilt_lower = (back_upper.astype(jnp.float32) - jax.nn.silu(pre_held)).astype(jnp.bfloat16)
    rebuilt = jnp.stack([back_lower, rebuilt_lower])[None]

    pre = project(shares(upper_in))
    upper_out = (lower_in.astype(jnp.float32) + jax.nn.silu(pre)).astype(jnp.bfloat16)
    emitted = jnp.stack([upper_out, upper_in])[None]

    terms = lax.dot_general(
        hidden_all, own_weight, (((1,), (1,)), ((), ())), preferred_element_type=jnp.float32
    ).astype(jnp.bfloat16)
    terms = lax.all_to_all(terms, "dp", split_axis=0, concat_axis=1, tiled=True)
    through = lax.psum_scatter(terms, "tensor", scatter_dimension=1, tiled=True).astype(jnp.float32)
    dupper_in = (dlower.astype(jnp.float32) + through).astype(jnp.bfloat16)
    grads_out = jnp.stack([dupper_in, dupper])[None]
    weight_grad = across_rows(held_share, hidden_all).astype(jnp.bfloat16)[None]
    return (emitted, rebuilt, grads_out, weight_grad)


MESH = pl.DeviceIdType.MESH
BACK_LOWER, GRAD_UPPER, BACK_UPPER, GRAD_LOWER, OUT_UPPER, OUT_LOWER = range(6)


def step_kernel(
    lengths, sent_out, sent_back, sent_grad, weight,
    emitted, rebuilt, grads_out, weight_grad,
    w, got, share, part, summed, hidden, terms, tx, trx, ts, tr, stage, wg,
    z_send, z_recv, b_send, b_recv, d_send, d_recv, r_send, r_recv, p_send, p_recv,
    h_send, h_recv, t_send, t_recv, f_send, f_recv, w_sem, o_sem,
):
    f32, bf16 = jnp.float32, jnp.bfloat16
    n_s, n_d, n_t = (lax.axis_size(a) for a in ("section", "dp", "tensor"))
    me_s, me_d, me_t = (lax.axis_index(a) for a in ("section", "dp", "tensor"))
    rows, local_features = got.shape[1], got.shape[2]
    half, depth = share.shape[3], share.shape[4]
    per = local_features // depth
    other = 1 - me_t
    nxt, prv = lax.rem(me_s + 1, n_s), lax.rem(me_s + n_s - 1, n_s)

    def replica(k):
        return lax.rem(me_d + k + n_d, n_d)

    side = lax.rem(me_d, 2)
    x_near = me_d + 1 - 2 * side
    y_near = lax.rem(me_d + 2, n_d)
    far = lax.rem(x_near + 2, n_d)

    barrier = pltpu.get_barrier_semaphore()
    for k in range(n_d):
        for c in range(n_t):
            if k or c:
                pl.semaphore_signal(
                    barrier, inc=1, device_id=(me_s, replica(k), lax.rem(me_t + c, n_t)), device_id_type=MESH
                )
    for z in (nxt, prv):
        pl.semaphore_signal(barrier, inc=1, device_id=(z, me_d, me_t), device_id_type=MESH)
    pl.semaphore_wait(barrier, n_d * n_t - 1 + 2)

    def remote(src, dst, send, recv, where):
        return pltpu.make_async_remote_copy(
            src_ref=src, dst_ref=dst, send_sem=send, recv_sem=recv, device_id=where, device_id_type=MESH
        )

    def landed(dst, sem):
        pltpu.make_async_copy(dst, dst, sem).wait()

    def along_z(i):
        src, piece, z = {
            BACK_LOWER: (sent_back, 1, prv), BACK_UPPER: (sent_back, 0, prv),
            GRAD_UPPER: (sent_grad, 0, prv), GRAD_LOWER: (sent_grad, 1, prv),
            OUT_UPPER: (sent_out, 0, nxt), OUT_LOWER: (sent_out, 1, nxt),
        }[i]
        return remote(src.at[0, piece], got.at[i], z_send.at[i], z_recv.at[i], (z, me_d, me_t))

    def back_lower(n):
        h, j = n // per, n % per
        piece = (pl.ds(h * half, half), pl.ds(j * depth, depth))
        return remote(
            sent_back.at[0, 1, *piece], got.at[BACK_LOWER, *piece], b_send.at[n], b_recv.at[n], (prv, me_d, me_t)
        )

    for n in range(n_t * per):
        back_lower(n).start()
    w_copy = pltpu.make_async_copy(weight.at[0], w, w_sem)
    w_copy.start()

    def deal(i, x, finish):
        for h in range(n_t):
            for j in range(per):
                n = h * per + j
                if i == BACK_LOWER and not finish:
                    back_lower(n).wait_recv()
                target = me_t * per + j
                src = got.at[i, pl.ds(h * half, half), pl.ds(j * depth, depth)]
                dst = share.at[x, me_d, h]
                own = jnp.logical_and(target == me_d, me_t == h)

                @pl.when(own)
                def _():
                    if not finish:
                        pltpu.make_async_copy(src, dst, d_recv.at[x, me_d]).start()

                @pl.when(jnp.logical_not(own))
                def _():
                    copy = remote(src, dst, d_send.at[x, n], d_recv.at[x, me_d], (me_s, target, h))
                    if finish:
                        copy.wait_send()
                    else:
                        copy.start()

    def relay(x, k):
        r = replica(k)
        return remote(
            share.at[x, r, me_t], share.at[x, r, me_t], r_send.at[x, r], r_recv.at[x, r], (me_s, me_d, other)
        )

    wide = local_features // 2

    def partial(x, n):
        r, side_of, target = (
            (far, 0, x_near), (far, 1, y_near), (x_near, 0, x_near),
            (y_near, 1, y_near), (y_near, 0, y_near), (x_near, 1, x_near),
        )[n]
        return remote(
            part.at[x, r, :, pl.ds(side_of * wide, wide)], summed.at[x, n],
            p_send.at[x, n], p_recv.at[x, n], (me_s, target, me_t),
        )

    def combine(x):
        for n in range(2):
            r = (y_near, x_near)[n]
            partial(x, n).wait_recv()
            for c in range(wide // 256):
                near = pl.ds(c * 256, 256)
                cols = pl.ds(n * wide + c * 256, 256)
                both = part[x, r, :, cols].astype(f32) + summed[x, n, :, near].astype(f32)
                part[x, r, :, cols] = both.astype(bf16)
            partial(x, n + 4).start()

    def gather(x):
        for k in range(n_d):
            landed(share.at[x, replica(k), me_t], d_recv.at[x, replica(k)])
            relay(x, k).start()
        for k in range(n_d):
            landed(share.at[x, replica(k), other], r_recv.at[x, replica(k)])

    def multiply(x):
        for k, r in enumerate((far, x_near, y_near, me_d)):

            @pl.loop(0, local_features // 512)
            def _(c):
                cols = pl.ds(pl.multiple_of(c * 512, 512), 512)
                left = share[x, r].reshape(rows, depth)
                part[x, r, :, cols] = jnp.dot(left, w[:, cols], preferred_element_type=f32).astype(bf16)

            for n in ((0, 1), (2,), (3,), ())[k]:
                partial(x, n).start()

    def total(x, c):
        cols = pl.ds(pl.multiple_of(c * 256, 256), 256)
        n = lax.div(c, wide // 256)
        near = pl.ds(pl.multiple_of(lax.rem(c, wide // 256) * 256, 256), 256)
        pre = part[x, me_d, :, cols].astype(f32)
        return pre + summed[x, 2 + n, :, near].astype(f32) + summed[x, 4 + n, :, near].astype(f32)

    def tiles(body):
        @pl.loop(0, local_features // 256)
        def _(c):
            body(c, pl.ds(pl.multiple_of(c * 256, 256), 256))

    def out(i, src, dst):
        return pltpu.make_async_copy(src, dst, o_sem.at[i])

    outs = [
        out(0, got.at[BACK_LOWER], rebuilt.at[0, 0]),
        out(1, got.at[OUT_UPPER], emitted.at[0, 1]),
        out(2, stage.at[0], grads_out.at[0, 1]),
        out(3, stage.at[1], rebuilt.at[0, 1]),
        out(4, stage.at[2], emitted.at[0, 0]),
        out(5, stage.at[3], grads_out.at[0, 0]),
        out(6, wg, weight_grad.at[0]),
    ]

    deal(BACK_LOWER, 0, False)
    along_z(GRAD_UPPER).start()
    outs[0].start()
    gather(0)
    w_copy.wait()
    multiply(0)
    along_z(GRAD_UPPER).wait_recv()
    along_z(OUT_UPPER).start()
    combine(0)
    for n in range(2, 6):
        partial(0, n).wait_recv()
    live = lengths[0, 0]

    def keep(block):
        place = lax.broadcasted_iota(jnp.int32, block.shape, 0)
        return jnp.where(place < live, block.astype(f32), 0.0)

    def hide(c, cols):
        pre = total(0, c)
        dupper = keep(got[GRAD_UPPER, :, cols])
        stage[0, :, cols] = dupper.astype(bf16)
        sigma = jax.nn.sigmoid(pre)
        gated = (dupper * (sigma * (1.0 + pre * (1.0 - sigma)))).astype(bf16)
        hidden[me_d, :, :, cols] = gated.reshape(n_t, half, 256)

    tiles(hide)

    def show(n):
        r, h, target = (
            (me_d, 0, x_near), (me_d, 1, y_near), (me_d, 1, x_near),
            (me_d, 0, y_near), (x_near, 0, y_near), (y_near, 1, x_near),
        )[n]
        block = hidden.at[r, h]
        return remote(block, block, h_send.at[n], h_recv.at[n], (me_s, target, me_t))

    def shown(n):
        r, h = ((x_near, 0), (y_near, 1), (x_near, 1), (y_near, 0), (far, 0), (far, 1))[n]
        landed(hidden.at[r, h], h_recv.at[n])

    for n in range(4):
        show(n).start()
    along_z(OUT_UPPER).wait_recv()
    along_z(BACK_UPPER).start()
    along_z(OUT_LOWER).start()
    along_z(GRAD_LOWER).start()
    deal(OUT_UPPER, 1, False)
    outs[1].start()
    for n in range(2):
        shown(n)
        show(n + 4).start()
    gather(1)
    multiply(1)
    outs[2].start()

    along_z(BACK_UPPER).wait_recv()

    def rebuild(c, cols):
        pre = total(0, c)
        upper = got[BACK_UPPER, :, cols].astype(f32)
        stage[1, :, cols] = (upper - pre * jax.nn.sigmoid(pre)).astype(bf16)

    tiles(rebuild)
    outs[3].start()

    for n in range(2, 6):
        shown(n)

    @pl.loop(0, depth // 256)
    def _(c):
        cols = pl.ds(pl.multiple_of(c * 256, 256), 256)
        left = hidden[...].reshape(n_d * rows, local_features)
        product = lax.dot_general(left, w[cols, :], (((1,), (1,)), ((), ())), preferred_element_type=f32)
        terms[:, :, :, cols] = product.reshape(n_d, n_t, half, 256)

    for r in range(n_d):
        tx[r] = terms[r, other].astype(bf16)
    swap = remote(tx, trx, t_send, t_recv, (me_s, me_d, other))
    swap.start()
    combine(1)

    def weigh(lo, hi):
        @pl.loop(lo, hi)
        def _(c):
            cols = pl.ds(pl.multiple_of(c * 256, 256), 256)
            left = share[0, :, :, :, cols].reshape(n_d * rows, 256)
            right = hidden[...].reshape(n_d * rows, local_features)
            product = lax.dot_general(left, right, (((0,), (0,)), ((), ())), preferred_element_type=f32)
            wg[cols, :] = product.astype(bf16)

    swap.wait_recv()
    owner, place = lax.div(me_d, per), lax.rem(me_d, per)

    def back_to(k, finish):
        r = replica(k)
        src, dst = ts.at[r], tr.at[place, me_t]
        own = jnp.logical_and(k == 0, me_t == owner)

        @pl.when(own)
        def _():
            if not finish:
                pltpu.make_async_copy(src, dst, f_recv.at[place, me_t]).start()

        @pl.when(jnp.logical_not(own))
        def _():
            copy = remote(src, dst, f_send.at[k], f_recv.at[place, me_t], (me_s, r, owner))
            if finish:
                copy.wait_send()
            else:
                copy.start()

    for k in range(1, n_d + 1):
        r = replica(k)
        ts[r] = (terms[r, me_t] + trx[r].astype(f32)).astype(bf16)
        back_to(k % n_d, False)

    weigh(0, depth // 256)
    outs[6].start()

    along_z(OUT_LOWER).wait_recv()
    for n in range(2, 6):
        partial(1, n).wait_recv()

    def emit(c, cols):
        pre = total(1, c)
        lower = got[OUT_LOWER, :, cols].astype(f32)
        stage[2, :, cols] = (lower + pre * jax.nn.sigmoid(pre)).astype(bf16)

    tiles(emit)
    outs[4].start()

    along_z(GRAD_LOWER).wait_recv()
    for j in range(per):
        for h in range(n_t):
            landed(tr.at[j, h], f_recv.at[j, h])

    for j in range(per):
        span = pl.ds(j * depth, depth)
        through = tr[j].reshape(rows, depth).astype(f32)
        stage[3, :, span] = (keep(got[GRAD_LOWER, :, span]) + through).astype(bf16)
    outs[5].start()

    for n in range(n_t * per):
        back_lower(n).wait_send()
    for i in range(1, 6):
        along_z(i).wait_send()
    for x, i in ((0, BACK_LOWER), (1, OUT_UPPER)):
        deal(i, x, True)
        for k in range(n_d):
            relay(x, k).wait_send()
        for n in range(6):
            partial(x, n).wait_send()
    for n in range(6):
        show(n).wait_send()
    swap.wait_send()
    for k in range(n_d):
        back_to(k, True)
    for copy in outs:
        copy.wait()


def together(sizes, sent_out, sent_back, sent_grad, lengths, weight):
    n_d, n_t = sizes
    rows, features = sent_out.shape[2:]
    depth = weight.shape[1]
    half, per = rows // n_t, features // depth
    bf16 = jnp.bfloat16
    dma, vmem = pltpu.SemaphoreType.DMA, pltpu.VMEM
    anywhere = pl.BlockSpec(memory_space=pl.ANY)
    return pl.pallas_call(
        step_kernel,
        out_shape=[jax.ShapeDtypeStruct(a.shape, bf16) for a in (sent_out, sent_back, sent_grad, weight)],
        in_specs=[pl.BlockSpec(memory_space=pltpu.SMEM)] + [anywhere] * 4,
        out_specs=[anywhere] * 4,
        scratch_shapes=[
            vmem((depth, features), bf16),
            vmem((6, rows, features), bf16),
            vmem((2, n_d, n_t, half, depth), bf16),
            vmem((2, n_d, rows, features), bf16),
            vmem((2, 6, rows, features // 2), bf16),
            vmem((n_d, n_t, half, features), bf16),
            vmem((n_d, n_t, half, depth), jnp.float32),
            vmem((n_d, half, depth), bf16),
            vmem((n_d, half, depth), bf16),
            vmem((n_d, half, depth), bf16),
            vmem((per, n_t, half, depth), bf16),
            vmem((4, rows, features), bf16),
            vmem((depth, features), bf16),
            dma((6,)), dma((6,)),
            dma((n_t * per,)), dma((n_t * per,)),
            dma((2, n_t * per)), dma((2, n_d)),
            dma((2, n_d)), dma((2, n_d)),
            dma((2, 6)), dma((2, 6)),
            dma((6,)), dma((6,)),
            dma(()), dma(()),
            dma((n_d,)), dma((per, n_t)),
            dma(()), dma((7,)),
        ],
        compiler_params=pltpu.CompilerParams(
            collective_id=0, has_side_effects=True, vmem_limit_bytes=50 * 2**20
        ),
    )(lengths, sent_out, sent_back, sent_grad, weight)


def local(sizes, sent_out, sent_back, sent_grad, lengths, weight):
    n_s, n_d, n_t = sizes
    rows, features = sent_out.shape[2:]
    depth = weight.shape[1]
    fits = n_s > 2 and n_d == 4 and n_t == 2 and rows % 32 == 0 and features % depth == 0 and depth % 256 == 0
    if fits and features % 512 == 0:
        return tuple(together((n_d, n_t), sent_out, sent_back, sent_grad, lengths, weight))
    return spread(sent_out, sent_back, sent_grad, lengths, weight)


def solution(mesh):
    return jax.shard_map(
        functools.partial(local, tuple(mesh.shape[a] for a in ("section", "dp", "tensor"))),
        mesh=mesh,
        in_specs=(
            P("section", None, "dp", "tensor"),
            P("section", None, "dp", "tensor"),
            P("section", None, "dp", "tensor"),
            P("section", "dp"),
            P("section", "dp", "tensor"),
        ),
        out_specs=(
            P("section", None, "dp", "tensor"),
            P("section", None, "dp", "tensor"),
            P("section", None, "dp", "tensor"),
            P("section", "dp", "tensor"),
        ),
        check_vma=False,
    )
```
